256 devices in a mesh: rad: 4 (over x_hi, core), lat: 64 (over x_lo, z, y).
Axes of the slice: x: 4 (x_hi: 2, x_lo: 2; x = x_hi * 2 + x_lo), y: 4, z: 8, core: 2. Of those that a mesh axis runs over, the one named last changes fastest.
Arguments:
- velocity: bfloat16 [3, 128, 768, 1536], P(None, 'rad', 'lat'), may hold values from -6 to 6
- density: float32 [128], P('rad'), may hold values from 0.3 to 3
- offsets: int32 [4], replicated, may hold values from -3 to 3, as said below
- radial_weights: float32 [2, 4, 128], P(None, None, 'rad'), may hold values from -3 to 3
- angular_scale: float32 [128], P('rad'), may hold values from 9.536743e-07 to 3.8146973e-06
- order_table: int32 [512], replicated, may hold values from 0 to 511, as said below
- eigenfunctions: float32 [512, 32, 128], P(None, None, 'rad'), may hold values from -0.5 to 0.5
Outputs:
- coeffs: float32 [512, 2, 32, 512], P('lat', None, 'rad')
The draws below stay inside these ranges and needn't reach their ends.
Inputs may be any that keep to these rules, and one draw needn't show every extreme that they name: 4 distinct offsets; minus 3 and 3 are among them. `order_table`: a permutation of the orders; for every k, slots 2k and 2k + 1 hold orders m and 511 - m.
All inputs are finite; a program needn't handle non-finite values.
Results may differ from the reference program's by a relative error of at most 0.0003.
Values sent between devices are 32-bit elements; how exact they have to be, the bound alone decides.
No kernel may reach another device: no remote copies, remote signals or barrier semaphores. Data moves between devices by JAX's collectives and lax.ppermute only.
A program may use at most 128 MiB of HBM per device.

```python
import math
import jax
import jax.numpy as jnp
from jax import lax

NLON = 1536
NLAT = 768
LDEG = 512
NMODE = 32
TAPS = 4
HALO = 3
NR = 128


def draw_offsets(key, part):
    first, second = jax.random.split(jax.random.fold_in(key, 11))
    inner = jax.random.permutation(first, 2 * HALO - 1)[:TAPS - 2].astype(jnp.int32) - (HALO - 1)
    taps = jnp.concatenate([jnp.array([-HALO, HALO], jnp.int32), inner])
    return jax.random.permutation(second, taps)


def draw_order_table(key, part):
    first, second = jax.random.split(jax.random.fold_in(key, 23))
    pairs = jax.random.permutation(first, LDEG // 2).astype(jnp.int32)
    flips = jax.random.randint(second, (LDEG // 2,), 0, 2, dtype=jnp.int32)
    lower = jnp.where(flips == 1, LDEG - 1 - pairs, pairs)
    upper = LDEG - 1 - lower
    return jnp.stack([lower, upper], axis=1).reshape(LDEG)


def block_scale(stream_key, extent, shards, least, top_value):
    def one(position, parts):
        draws = jax.random.uniform(jax.random.fold_in(jax.random.fold_in(stream_key, 6), position), (parts,), jnp.float32, least / len(shards), top_value / len(shards))
        return jnp.repeat(jnp.exp(draws), extent[position] // parts).reshape((-1,) + (1,) * (len(extent) - position - 1))

    loudness = one(*shards[0])
    for cut in shards[1:]:
        loudness = loudness * one(*cut)
    return loudness


def scatter_about(own_key, shape, deviation, most, shards=(), kind=jnp.bfloat16):
    values = deviation * jax.random.normal(own_key, shape, jnp.float32)
    if shards:
        values = values * block_scale(own_key, shape, shards, -0.22, 0.18)
    return jnp.clip(values, -most, most).astype(kind)


def setup_inputs(seed: int = 0) -> dict:
    splits = jax.random.split(jax.random.key(seed), 8)
    velocity = scatter_about(splits[0], (3, NR, NLAT, NLON), 1.0, 6.0, ((1, 4), (2, 64)))
    density = jnp.clip(jnp.exp(math.log(3.0) - 2.3025851 * jax.random.uniform(splits[1], (NR,), jnp.float32) ** block_scale(splits[1], (NR,), ((0, 4),), -0.2, 0.2)), 0.3, 3.0)
    offsets = draw_offsets(jax.random.fold_in(splits[7], 71), 0)
    radial_weights = scatter_about(splits[3], (2, TAPS, NR), 0.5, 3.0, ((2, 4),), jnp.float32)
    angular_scale = jnp.clip(jnp.exp(math.log(3.814697265625e-06) - 1.3862944 * jax.random.uniform(splits[4], (NR,), jnp.float32) ** block_scale(splits[4], (NR,), ((0, 4),), -0.2, 0.2)), 9.5367431640625e-07, 3.814697265625e-06)
    order_table = draw_order_table(jax.random.fold_in(splits[7], 71), 0)
    eigenfunctions = scatter_about(splits[6], (LDEG, NMODE, NR), NR ** -0.5, 0.5, ((2, 4),), jnp.float32)
    return dict(velocity=velocity, density=density, offsets=offsets, radial_weights=radial_weights, angular_scale=angular_scale, order_table=order_table, eigenfunctions=eigenfunctions)


def legendre_rows(orders, lat_count, degrees):
    colatitude = jnp.pi * (jnp.arange(lat_count, dtype=jnp.float32) + 0.5) / lat_count
    cosine = jnp.cos(colatitude)
    sine = jnp.sin(colatitude)
    order_float = orders.astype(jnp.float32)
    ladder = jnp.arange(1, degrees, dtype=jnp.float32)
    log_steps = jnp.concatenate([jnp.zeros((1,), jnp.float32), jnp.cumsum(0.5 * jnp.log((2.0 * ladder + 1.0) / (2.0 * ladder)))])
    log_start = 0.5 * jnp.log(jnp.ones((), jnp.float32) * 0.5) + jnp.take(log_steps, orders)
    log_diagonal = log_start[:, None] + order_float[:, None] * jnp.log(sine)[None, :]

    def advance(state, degree):
        previous, older, exponent = state
        level = degree.astype(jnp.float32)
        upward = jnp.sqrt((4.0 * level * level - 1.0) / jnp.maximum(level * level - order_float * order_float, 1.0))
        backward = jnp.sqrt(jnp.maximum((level - 1.0) * (level - 1.0) - order_float * order_float, 0.0) / jnp.maximum(4.0 * (level - 1.0) * (level - 1.0) - 1.0, 1.0))
        recurred = upward[:, None] * (cosine[None, :] * previous - backward[:, None] * older)
        starting = (degree == orders)[:, None]
        scaled = jnp.where(starting, jnp.ones_like(recurred), jnp.where((degree > orders)[:, None], recurred, jnp.zeros_like(recurred)))
        exponent = jnp.where(starting, log_diagonal, exponent)
        ratio = jnp.maximum(jnp.abs(scaled), 1.0)
        scaled = scaled / ratio
        previous = previous / ratio
        exponent = exponent + jnp.log(ratio)
        return ((scaled, previous, exponent), (scaled, exponent))
    zeros = jnp.zeros((orders.shape[0], lat_count), jnp.float32)
    _, outputs = lax.scan(advance, (zeros, zeros, zeros), jnp.arange(degrees, dtype=jnp.int32), unroll=32)
    rows = outputs[0] * jnp.exp(outputs[1])
    weight = jnp.sqrt(jnp.pi / lat_count) * sine
    return rows * weight[None, None, :]

def spectral_source(part, rows):
    transformed = jnp.einsum('fijco,loj->fiocl', part, rows, precision=lax.Precision.HIGHEST)
    level = jnp.arange(rows.shape[0], dtype=jnp.float32)
    degree_factor = level * (level + 1.0)
    return transformed[0] - degree_factor * transformed[1]

def grid_fields(flow, density, padded, offsets, radial_weights, angular_scale):
    radial, polar, azimuth = (flow[0], flow[1], flow[2])
    rho = density[:, None, None]
    shells = flow.shape[1]
    radial_term = jnp.zeros_like(radial)
    for tap in range(TAPS):
        shifted = lax.dynamic_slice_in_dim(padded, (HALO + offsets[tap]).astype(jnp.int32), shells, 1)
        radial_term = radial_term + radial_weights[0, tap][:, None, None] * shifted[0] + radial_weights[1, tap][:, None, None] * shifted[1]
    angular_term = angular_scale[:, None, None] * rho * (polar * polar + azimuth * azimuth - 2.0 * radial * radial + polar * azimuth)
    return (radial_term, angular_term)

def reference(velocity, density, offsets, radial_weights, angular_scale, order_table, eigenfunctions):
    lat_block = math.gcd(NLAT, 16)
    lat_blocks = NLAT // lat_block

    def band(block):
        flow = lax.dynamic_slice_in_dim(velocity, block * lat_block, lat_block, 2).astype(jnp.float32)
        rho = density[:, None, None]
        cross = jnp.stack([rho * flow[0] * flow[1], rho * flow[0] * flow[2]])
        padded = jnp.pad(cross, ((0, 0), (HALO, HALO), (0, 0), (0, 0)))
        radial_term, angular_term = grid_fields(flow, density, padded, offsets, radial_weights, angular_scale)
        fields = jnp.stack([radial_term, angular_term])
        waves = jnp.fft.rfft(fields, axis=-1)[..., :LDEG] / jnp.sqrt(jnp.ones((), jnp.float32) * NLON)
        return jnp.stack([jnp.real(waves), jnp.imag(waves)], axis=3)
    bands = lax.map(band, jnp.arange(lat_blocks, dtype=jnp.int32))
    spectrum = jnp.moveaxis(bands, 0, 2).reshape(2, NR, NLAT, 2, LDEG)
    order_block = 16

    def order_group(block):
        orders = (block * order_block + jnp.arange(order_block, dtype=jnp.int32)).astype(jnp.int32)
        rows = legendre_rows(orders, NLAT, LDEG)
        part = lax.dynamic_slice_in_dim(spectrum, block * order_block, order_block, 4)
        source = spectral_source(part, rows)
        return jnp.einsum('rocl,lnr->ocnl', source, eigenfunctions, precision=lax.Precision.HIGHEST)
    natural = lax.map(order_group, jnp.arange(LDEG // order_block, dtype=jnp.int32))
    natural = natural.reshape(LDEG, 2, NMODE, LDEG)
    return jnp.take(natural, order_table, axis=0)
```

```python
import functools
import math

import jax
import jax.numpy as jnp
import numpy as np
from jax import lax
from jax.experimental import pallas as pl
from jax.experimental.pallas import tpu as pltpu
from jax.sharding import PartitionSpec as P

TAPS = 4
HALO = 3
LANES = 128
LEVEL = 60.0


def master_tables(lon, degrees):
    half = lon // 2
    orders = np.arange(degrees).reshape(degrees // 2, 2).T
    angle = (2.0 * np.pi / lon) * ((orders[:, :, None] * np.arange(half)) % lon)
    full = np.stack([np.cos(angle), -np.sin(angle)], axis=1) / math.sqrt(lon)
    high = full.astype(np.float32).astype(jnp.bfloat16)
    low = (full - high.astype(np.float64)).astype(np.float32).astype(jnp.bfloat16)
    return np.concatenate([high, low], axis=1)


def split(x):
    high = x.astype(jnp.bfloat16)
    return high, (x - high.astype(jnp.float32)).astype(jnp.bfloat16)


def gather_kernel(row_ref, table_ref, out_ref):
    count = table_ref.shape[2]
    hot = row_ref[0] == lax.broadcasted_iota(jnp.int32, (count, count), 1)
    out_ref[0, 0] = jnp.dot(
        hot.astype(jnp.bfloat16), table_ref[0, 0], preferred_element_type=jnp.float32
    ).astype(jnp.bfloat16)


def gathered_tables(rows, tables):
    _, kinds, count, half = tables.shape
    return pl.pallas_call(
        gather_kernel,
        grid=(2, kinds),
        in_specs=[
            pl.BlockSpec((1, count, 1), lambda p, k: (p, 0, 0)),
            pl.BlockSpec((1, 1, count, half), lambda p, k: (p, k, 0, 0)),
        ],
        out_specs=pl.BlockSpec((1, 1, count, half), lambda p, k: (p, k, 0, 0)),
        out_shape=jax.ShapeDtypeStruct(tables.shape, jnp.bfloat16),
        name="gather_rows",
    )(rows[:, :, None], tables)


def fourier_kernel(
    off_ref, rho_ref, w_ref, ang_ref, v_ref, lo_ref, hi_ref, t_ref, y_ref, c_ref, g_ref
):
    shells, lats, lon = v_ref.shape[1:]
    half = lon // 2
    pitch = 16
    step = half // 2
    c_ref[:, 0:HALO] = lo_ref[...]
    c_ref[:, HALO + shells :] = hi_ref[...]

    def store_folded(field, r, col, a, b):
        rows = pl.ds(pl.multiple_of(r * pitch, pitch), lats)
        for i in range(step // LANES):
            lane = slice(i * LANES, (i + 1) * LANES)
            g_ref[0, field, col * (step // LANES) + i, rows] = (a + b)[:, lane]
            g_ref[1, field, col * (step // LANES) + i, rows] = (a - b)[:, lane]

    def first(r, _):
        rho = rho_ref[r]
        scale = ang_ref[r] * rho
        for col in range(2):
            terms = []
            for part in range(2):
                cols = slice(part * half + col * step, part * half + (col + 1) * step)
                radial = v_ref[0, r, :, cols].astype(jnp.float32)
                polar = v_ref[1, r, :, cols].astype(jnp.float32)
                azimuth = v_ref[2, r, :, cols].astype(jnp.float32)
                flux = rho * radial
                c_ref[0, r + HALO, :, cols] = flux * polar
                c_ref[1, r + HALO, :, cols] = flux * azimuth
                terms.append(
                    scale
                    * (
                        polar * polar
                        + azimuth * azimuth
                        - 2.0 * radial * radial
                        + polar * azimuth
                    )
                )
            store_folded(1, r, col, *terms)
        return 0

    lax.fori_loop(0, shells, first, 0)

    def second(r, _):
        for col in range(2):
            terms = []
            for part in range(2):
                cols = slice(part * half + col * step, part * half + (col + 1) * step)
                total = jnp.zeros((lats, step), jnp.float32)
                for tap in range(TAPS):
                    at = r + HALO + off_ref[tap]
                    total = (
                        total
                        + w_ref[0, tap, r] * c_ref[0, at, :, cols]
                        + w_ref[1, tap, r] * c_ref[1, at, :, cols]
                    )
                terms.append(total)
            store_folded(0, r, col, *terms)
        return 0

    lax.fori_loop(0, shells, second, 0)

    count = t_ref.shape[2]
    group = 4
    nt = (((1,), (1,)), ((), ()))
    upper = (lax.broadcasted_iota(jnp.int32, (count, LANES), 0) & 7) < 4
    for block in range(lats // group):
        sums = []
        for parity in range(2):
            rows = []
            for j in range(block * group, (block + 1) * group):
                for field in range(2):
                    rows.append(
                        jnp.concatenate(
                            [
                                g_ref[parity, field, i, pl.ds(j, shells, stride=pitch), :]
                                for i in range(half // LANES)
                            ],
                            axis=1,
                        )
                    )
            high, low = split(jnp.concatenate(rows, axis=0))
            table = t_ref[parity].reshape(4 * count, half)
            main = lax.dot_general(table, high, nt, preferred_element_type=jnp.float32)
            rest = lax.dot_general(
                table[: 2 * count], low, nt, preferred_element_type=jnp.float32
            )
            sums.append(main[: 2 * count] + main[2 * count :] + rest)
        for j in range(group):
            cols = slice(j * 64, (j + 1) * 64)
            even, odd = (
                jnp.concatenate([s[:count, cols], s[count:, cols]], axis=1) for s in sums
            )
            tiles = (count // 8, 8, LANES)
            y_ref[:, 0, block * group + j] = jnp.where(upper, even, odd).reshape(tiles)
            y_ref[:, 1, block * group + j] = jnp.where(upper, odd, even).reshape(tiles)


def fourier(offsets, density, weights, angular, velocity, below, above, tables):
    _, shells, lats, lon = velocity.shape
    count = tables.shape[2]
    smem = pl.BlockSpec(memory_space=pltpu.SMEM)
    vmem = pl.BlockSpec(memory_space=pltpu.VMEM)
    return pl.pallas_call(
        fourier_kernel,
        in_specs=[smem] * 4 + [vmem] * 4,
        out_specs=vmem,
        out_shape=jax.ShapeDtypeStruct((count // 8, 2, lats, 8, LANES), jnp.float32),
        scratch_shapes=[
            pltpu.VMEM((2, shells + 2 * HALO, lats, lon), jnp.float32),
            pltpu.VMEM((2, 2, lon // 2 // LANES, shells * 16, LANES), jnp.float32),
        ],
        name="fourier",
    )(offsets, density, weights, angular, velocity, below, above, tables)


def legendre_kernel(inv_ref, m_ref, start_ref, trig_ref, out_ref, s_ref, p_ref, z_ref, e_ref, f_ref):
    block = out_ref.shape[1] // 8
    lat_count = trig_ref.shape[1]
    base = pl.program_id(0) * block
    wide = lat_count // LANES
    order = jnp.broadcast_to(m_ref[...], (8, LANES))
    quantum = LEVEL * math.log(2.0)

    def columns(i):
        return slice(i * LANES, (i + 1) * LANES)

    @pl.when(pl.program_id(0) == 0)
    def _():
        start = jnp.broadcast_to(start_ref[...], (8, LANES))
        for i in range(wide):
            log_value = start + order * trig_ref[1:2, columns(i)]
            level = jnp.minimum(jnp.ceil(log_value * (1.0 / quantum)), 0.0)
            z_ref[:, columns(i)] = (
                jnp.exp(log_value - level * quantum) * trig_ref[2:3, columns(i)]
            )
            e_ref[:, columns(i)] = level
        zero = jnp.zeros((8, lat_count), jnp.float32)
        s_ref[...] = zero
        p_ref[...] = zero

    def eight(chunk, _):
        levels, scales, current, older = [], [], [], []
        for i in range(wide):
            s = s_ref[:, columns(i)]
            p = p_ref[:, columns(i)]
            e = e_ref[:, columns(i)]
            grow = (jnp.maximum(jnp.abs(s), jnp.abs(p)) > 1.0) & (e < 0.0)
            shrink = jnp.where(grow, 2.0**-LEVEL, 1.0)
            e = e + jnp.where(grow, 1.0, 0.0)
            e_ref[:, columns(i)] = e
            current.append(s * shrink)
            older.append(p * shrink)
            scales.append(
                jnp.where(
                    e > -0.5,
                    1.0,
                    jnp.where(e > -1.5, 2.0**-LEVEL, jnp.where(e > -2.5, 2.0 ** (-2 * LEVEL), 0.0)),
                )
            )
        first = base + chunk * 8
        before = jnp.maximum(first - 1, 0)
        before_f = before.astype(jnp.float32)
        back = jnp.maximum((before_f * before_f - order * order) * inv_ref[before], 1e-7)
        back = jnp.sqrt(back)
        for step in range(8):
            degree = first + step
            level = degree.astype(jnp.float32)
            ratio = jnp.maximum((level * level - order * order) * inv_ref[degree], 1e-7)
            up = lax.rsqrt(ratio)
            up_back = up * back
            back = ratio * up
            starting = order == level
            for i in range(wide):
                entry = jnp.where(starting, z_ref[:, columns(i)], 0.0) - up_back * older[i]
                value = (up * trig_ref[0:1, columns(i)]) * current[i] + entry
                older[i] = current[i]
                current[i] = value
                row = pl.multiple_of((chunk * 8 + step) * 8, 8)
                out_ref[i, pl.ds(row, 8), :] = value * scales[i]
        for i in range(wide):
            s_ref[:, columns(i)] = current[i]
            p_ref[:, columns(i)] = older[i]
        return 0

    lax.fori_loop(0, block // 8, eight, 0)


def legendre_table(orders, lat_count, degrees):
    colatitude = np.pi * (np.arange(lat_count) + 0.5) / lat_count
    sine = np.sin(colatitude)
    trig = np.stack(
        [np.cos(colatitude), np.log(sine), math.sqrt(np.pi / lat_count) * sine]
    ).astype(np.float32)
    ladder = np.arange(1, degrees)
    logs = 0.5 * math.log(0.5) + np.concatenate(
        [[0.0], np.cumsum(0.5 * np.log((2.0 * ladder + 1.0) / (2.0 * ladder)))]
    )
    level = np.arange(degrees, dtype=np.float64)
    inverse = (1.0 / np.maximum(4.0 * level * level - 1.0, 1.0)).astype(np.float32)
    start = jnp.take(jnp.asarray(logs, jnp.float32), orders)[:, None]
    block = 64
    vmem = pl.BlockSpec(memory_space=pltpu.VMEM)
    return pl.pallas_call(
        legendre_kernel,
        grid=(degrees // block,),
        in_specs=[pl.BlockSpec(memory_space=pltpu.SMEM), vmem, vmem, vmem],
        out_specs=pl.BlockSpec((lat_count // LANES, block * 8, LANES), lambda i: (0, i, 0)),
        out_shape=jax.ShapeDtypeStruct((lat_count // LANES, degrees * 8, LANES), jnp.float32),
        scratch_shapes=[pltpu.VMEM((8, lat_count), jnp.float32)] * 5,
        name="legendre_table",
    )(inverse, orders.astype(jnp.float32)[:, None], start, trig)


def project_kernel(m_ref, slot_ref, z_ref, t_ref, e_ref, out_ref, s_ref):
    wide = t_ref.shape[0]
    block = t_ref.shape[1] // 8
    lat_count = wide * LANES
    shells, modes = e_ref.shape[:2]
    base = pl.program_id(0) * block
    degree = (base + lax.broadcasted_iota(jnp.int32, (block, LANES), 0)).astype(jnp.float32)
    factor = degree * (degree + 1.0)
    for o in range(8):
        active = m_ref[o] < base + block

        @pl.when(active)
        def _(o=o):
            data_high, data_low = split(z_ref[pl.ds(o, lat_count, stride=8), :])
            rows = jnp.concatenate(
                [t_ref[i, pl.ds(o, block, stride=8), :] for i in range(wide)],
                axis=1,
            )
            high, low = split(rows)
            both = jnp.dot(high, data_high, preferred_element_type=jnp.float32)
            both += jnp.dot(low, data_high, preferred_element_type=jnp.float32)
            both += jnp.dot(high, data_low, preferred_element_type=jnp.float32)
            other = pltpu.roll(both, LANES - shells, 1)
            s_ref[o] = (both - factor * other).T

        @pl.when(jnp.logical_not(active))
        def _(o=o):
            s_ref[o] = jnp.zeros((LANES, block), jnp.float32)

    def project(pair, _):
        totals = [[jnp.zeros((modes, block), jnp.float32) for _ in range(2)] for _ in range(2)]
        for r in range(shells):
            eigen = e_ref[r]
            for a in range(2):
                for part in range(2):
                    row = s_ref[pair * 2 + a, part * 2 * shells + r : part * 2 * shells + r + 1, :]
                    totals[a][part] = totals[a][part] + eigen * row
        quarter = modes // 4
        for a in range(2):
            slot = slot_ref[pair * 2 + a]
            for part in range(2):
                for q in range(4):
                    out_ref[q, slot, part] = totals[a][part][q * quarter : (q + 1) * quarter]
        return 0

    lax.fori_loop(0, 4, project, 0)


def projected(orders, slots, spectrum, table, eigen):
    wide = table.shape[0]
    lat_count = wide * LANES
    shells, modes, degrees = eigen.shape
    block = LANES
    smem = pl.BlockSpec(memory_space=pltpu.SMEM)
    return pl.pallas_call(
        project_kernel,
        grid=(degrees // block,),
        in_specs=[
            smem,
            smem,
            pl.BlockSpec(memory_space=pltpu.VMEM),
            pl.BlockSpec((wide, block * 8, LANES), lambda i: (0, i, 0)),
            pl.BlockSpec((shells, modes, block), lambda i: (0, 0, i)),
        ],
        out_specs=pl.BlockSpec((4, 8, 2, modes // 4, block), lambda i: (0, 0, 0, 0, i)),
        out_shape=jax.ShapeDtypeStruct((4, 8, 2, modes // 4, degrees), jnp.float32),
        scratch_shapes=[pltpu.VMEM((8, LANES, block), jnp.float32)],
        name="project",
    )(orders, slots, spectrum.reshape(lat_count * 8, LANES), table, eigen)


def body(velocity, density, offsets, radial_weights, angular_scale, order_table, eigenfunctions):
    shells, lats, lon = velocity.shape[1:]
    degrees = order_table.shape[0]
    groups = lax.axis_size("lat")
    lat_count = lats * groups
    where = lax.axis_index("lat")

    def cross(part):
        flow, rho = part
        flow = flow.astype(jnp.float32)
        flux = rho[:, None, None] * flow[0]
        return jnp.stack([flux * flow[1], flux * flow[2]])

    size = lax.axis_size("rad")
    up = [(i, i + 1) for i in range(size - 1)]
    down = [(j, i) for i, j in up]
    below = lax.ppermute(cross((velocity[:, shells - HALO :], density[shells - HALO :])), "rad", up)
    above = lax.ppermute(cross((velocity[:, :HALO], density[:HALO])), "rad", down)

    pairs = order_table.reshape(degrees // 2, 2)
    first_even = (pairs[:, 0] & 1) == 0
    even = jnp.where(first_even, pairs[:, 0], pairs[:, 1])
    odd = jnp.where(first_even, pairs[:, 1], pairs[:, 0])
    swapped = odd.reshape(-1, 2, 4)[:, ::-1].reshape(-1)
    tables = gathered_tables(jnp.stack([even, swapped]) >> 1, master_tables(lon, degrees))
    by_slot = fourier(
        offsets, density, radial_weights, angular_scale, velocity, below, above, tables
    )
    by_slot = by_slot.reshape(groups, lats, 8, LANES)
    gathered = lax.all_to_all(by_slot, "lat", split_axis=0, concat_axis=0, tiled=True)

    mine = lax.dynamic_slice_in_dim(pairs, where * 4, 4)
    flip = (mine[:, 0] & 1) ^ (where & 1)
    flip = flip[None, :] ^ jnp.arange(2, dtype=jnp.int32)[:, None]
    orders = jnp.where(flip == 0, mine[None, :, 0], mine[None, :, 1]).reshape(8)
    slots = (2 * jnp.arange(4, dtype=jnp.int32)[None, :] + flip).reshape(8)
    table = legendre_table(orders, lat_count, degrees)
    eigen = jnp.transpose(eigenfunctions, (2, 1, 0))
    partial = projected(orders, slots, gathered.reshape(lat_count, 8, LANES), table, eigen)
    return lax.all_to_all(partial, "rad", split_axis=0, concat_axis=0, tiled=True).sum(0)


def solution(mesh):
    placed = (
        P(None, "rad", "lat", None),
        P("rad"),
        P(),
        P(None, None, "rad"),
        P("rad"),
        P(),
        P(None, None, "rad"),
    )
    return jax.shard_map(
        body, mesh=mesh, in_specs=placed, out_specs=P("lat", None, "rad", None), check_vma=False
    )
```

```python
import functools
import math

import jax
import jax.numpy as jnp
import numpy as np
from jax import lax
from jax.experimental import pallas as pl
from jax.experimental.pallas import tpu as pltpu
from jax.sharding import PartitionSpec as P

TAPS = 4
HALO = 3
LANES = 128
LEVEL = 60.0


def master_tables(lon, degrees):
    half = lon // 2
    orders = np.arange(degrees).reshape(degrees // 2, 2).T
    angle = (2.0 * np.pi / lon) * ((orders[:, :, None] * np.arange(half)) % lon)
    full = np.stack([np.cos(angle), -np.sin(angle)], axis=1) / math.sqrt(lon)
    high = full.astype(np.float32).astype(jnp.bfloat16)
    low = (full - high.astype(np.float64)).astype(np.float32).astype(jnp.bfloat16)
    return np.concatenate([high, low], axis=1)


def split(x):
    high = x.astype(jnp.bfloat16)
    return high, (x - high.astype(jnp.float32)).astype(jnp.bfloat16)


def gather_kernel(first_ref, table_ref, out_ref):
    kinds, count = table_ref.shape[1:3]
    parity = pl.program_id(0)
    first = first_ref[...]
    even = jnp.where((first & 1) == 0, first, 2 * count - 1 - first)
    odd = 2 * count - 1 - even
    lane = lax.broadcasted_iota(jnp.int32, (1, count), 1)
    swapped = jnp.where((lane & 4) == 0, pltpu.roll(odd, count - 4, 1), pltpu.roll(odd, 4, 1))
    row = jnp.where(parity == 0, even, swapped) >> 1
    hot = (lax.broadcasted_iota(jnp.int32, (count, count), 0) == row).astype(jnp.float32)
    hot = hot.T.astype(jnp.bfloat16)
    for kind in range(kinds):
        out_ref[0, kind] = jnp.dot(
            hot, table_ref[0, kind], preferred_element_type=jnp.float32
        ).astype(jnp.bfloat16)


def gathered_tables(first, tables):
    block = pl.BlockSpec((1,) + tables.shape[1:], lambda p: (p, 0, 0, 0))
    return pl.pallas_call(
        gather_kernel,
        grid=(2,),
        in_specs=[pl.BlockSpec(memory_space=pltpu.VMEM), block],
        out_specs=block,
        out_shape=jax.ShapeDtypeStruct(tables.shape, jnp.bfloat16),
        name="gather_rows",
    )(first, tables)


def halo_kernel(rho_ref, v_ref, top_ref, bottom_ref, flow_ref, sem):
    lats, shells, lon = v_ref.shape[1:]
    starts = (shells - 8, 0)
    copies = [
        pltpu.make_async_copy(v_ref.at[:, :, pl.ds(start, 8)], flow_ref.at[i], sem.at[i])
        for i, start in enumerate(starts)
    ]
    for copy in copies:
        copy.start()
    wide = lon // LANES
    row = lax.broadcasted_iota(jnp.int32, (8, LANES), 0)
    for i, (start, out_ref) in enumerate(zip(starts, (top_ref, bottom_ref))):
        skip = 8 - HALO if i == 0 else 0
        rho = jnp.zeros((8, LANES), jnp.float32)
        for h in range(8):
            rho = jnp.where(row == h, rho_ref[start + h], rho)
        copies[i].wait()

        def band(lat, _, i=i, rho=rho, out_ref=out_ref, skip=skip):
            for c in range(wide):
                cols = slice(c * LANES, (c + 1) * LANES)
                radial, polar, azimuth = (
                    flow_ref[i, k, lat, :, cols].astype(jnp.float32) for k in range(3)
                )
                flux = rho * radial
                for k, value in enumerate((flux * polar, flux * azimuth)):
                    for h in range(HALO):
                        out_ref[k, h, pl.ds(lat * wide + c, 1)] = value[skip + h : skip + h + 1]
            return 0

        lax.fori_loop(0, lats, band, 0)


def halo_cross(density, velocity):
    _, lats, shells, lon = velocity.shape
    vmem = pl.BlockSpec(memory_space=pltpu.VMEM)
    shape = jax.ShapeDtypeStruct((2, HALO, lats * lon // LANES, LANES), jnp.float32)
    return pl.pallas_call(
        halo_kernel,
        in_specs=[pl.BlockSpec(memory_space=pltpu.SMEM), pl.BlockSpec(memory_space=pl.ANY)],
        out_specs=[vmem, vmem],
        out_shape=[shape, shape],
        scratch_shapes=[
            pltpu.VMEM((2, 3, lats, 8, lon), jnp.bfloat16),
            pltpu.SemaphoreType.DMA((2,)),
        ],
        name="halo_cross",
    )(density, velocity)


CHUNK = 2


def chunk_copy(v_ref, flow_ref, sem, i):
    part = pl.ds(i * CHUNK, CHUNK)
    return pltpu.make_async_copy(v_ref.at[:, part], flow_ref.at[:, part], sem.at[i])


def start_chunks(v_ref, flow_ref, sem):
    for i in range(v_ref.shape[1] // CHUNK):
        chunk_copy(v_ref, flow_ref, sem, i).start()


def wait_chunk(v_ref, flow_ref, sem, lat):
    @pl.when(lat % CHUNK == 0)
    def _():
        chunk_copy(v_ref, flow_ref, sem, lat // CHUNK).wait()


def shell_rows(count, value):
    row = lax.broadcasted_iota(jnp.int32, (8, LANES), 0)
    tiles = []
    for base in range(0, count, 8):
        tile = jnp.zeros((8, LANES), jnp.float32)
        for h in range(8):
            tile = jnp.where(row == h, value(base + h), tile)
        tiles.append(tile)
    return jnp.concatenate(tiles, axis=0)


def store_folded(g_ref, lat, shells, chunk, a, b):
    place = (lat & ~3) + ((lat & 1) << 1) + ((lat & 2) >> 1)
    rows = pl.ds(pl.multiple_of(place * shells, shells), shells)
    cols = slice(chunk * LANES, (chunk + 1) * LANES)
    for parity, value in enumerate((a + b, a - b)):
        high, low = split(value)
        g_ref[parity, 0, rows, cols] = high
        g_ref[parity, 1, rows, cols] = low


def transform(g_ref, t_ref, shells, lats, emit):
    kinds, count, half = t_ref.shape[1:]
    nt = (((1,), (1,)), ((), ()))
    row = lax.broadcasted_iota(jnp.int32, (count, LANES), 0)
    lane = lax.broadcasted_iota(jnp.int32, (count, LANES), 1)
    upper = (row & 7) < 4
    straight = (lane & shells) == 0
    for start, size in ((0, 8), (8, 4)):
        rows = slice(start * shells, (start + size) * shells)
        sums = []
        for parity in range(2):
            table = t_ref[parity].reshape(kinds * count, half)
            high, low = g_ref[parity, 0, rows], g_ref[parity, 1, rows]
            if size == 8:
                main = lax.dot_general(table, high, nt, preferred_element_type=jnp.float32)
                rest = lax.dot_general(
                    table[: 2 * count], low, nt, preferred_element_type=jnp.float32
                )
                sums.append(main[: 2 * count] + main[2 * count :] + rest)
            else:
                both = jnp.concatenate([high, low], axis=0)
                main = lax.dot_general(table, both, nt, preferred_element_type=jnp.float32)
                width = size * shells
                sums.append(
                    main[: 2 * count, :width]
                    + (main[: 2 * count, width:] + main[2 * count :, :width])
                )
        for base in range(0, size, 4):
            cols = slice(base * shells, base * shells + LANES)
            found = []
            for total in sums:
                cosine, sine = total[:count, cols], total[count:, cols]
                found.append(
                    (
                        jnp.where(straight, cosine, pltpu.roll(sine, shells, 1)),
                        jnp.where(straight, pltpu.roll(cosine, LANES - shells, 1), sine),
                    )
                )
            for i in range(2):
                even, odd = found[0][i], found[1][i]
                tiles = (count // 8, 8, LANES)
                emit(
                    (start + base) // 2 + i,
                    jnp.where(upper, even, odd).reshape(tiles),
                    jnp.where(upper, odd, even).reshape(tiles),
                )


def angular_kernel(rho_ref, ang_ref, v_ref, t_ref, a_ref, flow_ref, g_ref, sem):
    lats, shells, lon = v_ref.shape[1:]
    wide = lon // LANES
    start_chunks(v_ref, flow_ref, sem)
    scale = shell_rows(shells, lambda r: ang_ref[r] * rho_ref[r])

    def band(lat, _):
        wait_chunk(v_ref, flow_ref, sem, lat)
        for chunk in range(wide // 2):
            terms = []
            for c in (chunk, chunk + wide // 2):
                cols = slice(c * LANES, (c + 1) * LANES)
                radial, polar, azimuth = (
                    flow_ref[k, lat, :, cols].astype(jnp.float32) for k in range(3)
                )
                terms.append(
                    scale
                    * (
                        polar * polar
                        + azimuth * azimuth
                        - 2.0 * radial * radial
                        + polar * azimuth
                    )
                )
            store_folded(g_ref, lat, shells, chunk, *terms)
        return 0

    lax.fori_loop(0, lats, band, 0)

    def emit(pair, left, right):
        a_ref[:, 0, pair] = left
        a_ref[:, 1, pair] = right

    transform(g_ref, t_ref, shells, lats, emit)


def radial_kernel(
    off_ref, rho_ref, w_ref, v_ref, lo_ref, hi_ref, t_ref, a_ref, y_ref, flow_ref, w_rows, c_ref, g_ref, sem
):
    lats, shells, lon = v_ref.shape[1:]
    wide = lon // LANES
    plane = lats * wide
    start_chunks(v_ref, flow_ref, sem)
    rho = shell_rows(shells, lambda r: rho_ref[r])
    for tap in range(TAPS):
        for k in range(2):
            w_rows[k, tap] = shell_rows(shells, lambda r: w_ref[k, tap, r])

    def band(lat, _):
        wait_chunk(v_ref, flow_ref, sem, lat)
        for c in range(wide):
            cols = slice(c * LANES, (c + 1) * LANES)
            radial, polar, azimuth = (
                flow_ref[k, lat, :, cols].astype(jnp.float32) for k in range(3)
            )
            flux = rho * radial
            c_ref[0, c, 8 : 8 + shells] = flux * polar
            c_ref[1, c, 8 : 8 + shells] = flux * azimuth
            for k in range(2):
                at = pl.ds(k * HALO * plane + lat * wide + c, HALO, stride=plane)
                c_ref[k, c, 8 - HALO : 8] = lo_ref[at, :]
                c_ref[k, c, 8 + shells : 8 + shells + HALO] = hi_ref[at, :]
        for chunk in range(wide // 2):
            terms = []
            for c in (chunk, chunk + wide // 2):
                total = jnp.zeros((shells, LANES), jnp.float32)
                for tap in range(TAPS):
                    at = pl.ds(8 + off_ref[tap], shells)
                    total = (
                        total
                        + w_rows[0, tap] * c_ref[0, c, at, :]
                        + w_rows[1, tap] * c_ref[1, c, at, :]
                    )
                terms.append(total)
            store_folded(g_ref, lat, shells, chunk, *terms)
        return 0

    lax.fori_loop(0, lats, band, 0)

    near = lax.broadcasted_iota(jnp.int32, y_ref.shape[:1] + (8, LANES), 2) < LANES // 2

    def emit(pair, *both):
        for i, mine in enumerate(both):
            other = a_ref[:, i, pair]
            y_ref[:, i, 2 * pair] = jnp.where(near, mine, pltpu.roll(other, LANES // 2, 2))
            y_ref[:, i, 2 * pair + 1] = jnp.where(near, pltpu.roll(mine, LANES // 2, 2), other)

    transform(g_ref, t_ref, shells, lats, emit)


def fourier(offsets, density, weights, angular, velocity, below, above, tables):
    _, lats, shells, lon = velocity.shape
    count = tables.shape[2]
    smem = pl.BlockSpec(memory_space=pltpu.SMEM)
    vmem = pl.BlockSpec(memory_space=pltpu.VMEM)
    hbm = pl.BlockSpec(memory_space=pl.ANY)
    flow = pltpu.VMEM(velocity.shape, velocity.dtype)
    folded = pltpu.VMEM((2, 2, lats * shells, lon // 2), jnp.bfloat16)
    sems = pltpu.SemaphoreType.DMA((lats // CHUNK,))
    ready = pl.pallas_call(
        angular_kernel,
        in_specs=[smem, smem, hbm, vmem],
        out_specs=vmem,
        out_shape=jax.ShapeDtypeStruct((count // 8, 2, lats // 2, 8, LANES), jnp.float32),
        scratch_shapes=[flow, folded, sems],
        name="angular",
    )(density, angular, velocity, tables)
    return pl.pallas_call(
        radial_kernel,
        in_specs=[smem] * 3 + [hbm] + [vmem] * 4,
        out_specs=vmem,
        out_shape=jax.ShapeDtypeStruct((count // 8, 2, lats, 8, LANES), jnp.float32),
        scratch_shapes=[
            flow,
            pltpu.VMEM((2, TAPS, shells, LANES), jnp.float32),
            pltpu.VMEM((2, lon // LANES, shells + 16, LANES), jnp.float32),
            folded,
            sems,
        ],
        name="radial",
    )(
        offsets,
        density,
        weights,
        velocity,
        below.reshape(-1, LANES),
        above.reshape(-1, LANES),
        tables,
        ready,
    )


def legendre_kernel(inv_ref, m_ref, start_ref, trig_ref, out_ref, s_ref, p_ref, z_ref, e_ref, x_ref):
    block = x_ref.shape[1] // 8
    pairs = out_ref.shape[1]
    degrees = block * pl.num_programs(0)
    lat_count = trig_ref.shape[1]
    base = pl.program_id(0) * block
    wide = lat_count // LANES
    order = jnp.broadcast_to(m_ref[...], (8, LANES))
    quantum = LEVEL * math.log(2.0)

    def columns(i):
        return slice(i * LANES, (i + 1) * LANES)

    @pl.when(pl.program_id(0) == 0)
    def _():
        start = jnp.broadcast_to(start_ref[...], (8, LANES))
        for i in range(wide):
            log_value = start + order * trig_ref[1:2, columns(i)]
            level = jnp.minimum(jnp.ceil(log_value * (1.0 / quantum)), 0.0)
            z_ref[:, columns(i)] = (
                jnp.exp(log_value - level * quantum) * trig_ref[2:3, columns(i)]
            )
            e_ref[:, columns(i)] = level
        zero = jnp.zeros((8, lat_count), jnp.float32)
        s_ref[...] = zero
        p_ref[...] = zero

    def eight(chunk, _):
        levels, scales, current, older = [], [], [], []
        for i in range(wide):
            s = s_ref[:, columns(i)]
            p = p_ref[:, columns(i)]
            e = e_ref[:, columns(i)]
            grow = (jnp.maximum(jnp.abs(s), jnp.abs(p)) > 1.0) & (e < 0.0)
            shrink = jnp.where(grow, 2.0**-LEVEL, 1.0)
            e = e + jnp.where(grow, 1.0, 0.0)
            e_ref[:, columns(i)] = e
            current.append(s * shrink)
            older.append(p * shrink)
            scales.append(
                jnp.where(
                    e > -0.5,
                    1.0,
                    jnp.where(e > -1.5, 2.0**-LEVEL, jnp.where(e > -2.5, 2.0 ** (-2 * LEVEL), 0.0)),
                )
            )
        first = base + chunk * 8
        before = jnp.maximum(first - 1, 0)
        before_f = before.astype(jnp.float32)
        back = jnp.maximum((before_f * before_f - order * order) * inv_ref[before], 1e-7)
        back = jnp.sqrt(back)
        for step in range(8):
            degree = first + step
            level = degree.astype(jnp.float32)
            ratio = jnp.maximum((level * level - order * order) * inv_ref[degree], 1e-7)
            up = lax.rsqrt(ratio)
            up_back = up * back
            back = ratio * up
            starting = order == level
            for i in range(wide):
                entry = jnp.where(starting, z_ref[:, columns(i)], 0.0) - up_back * older[i]
                value = (up * trig_ref[0:1, columns(i)]) * current[i] + entry
                older[i] = current[i]
                current[i] = value
                x_ref[i, pl.ds(chunk * 8 + step, 8, stride=block), :] = value * scales[i]
        for i in range(wide):
            s_ref[:, columns(i)] = current[i]
            p_ref[:, columns(i)] = older[i]
        return 0

    lax.fori_loop(0, block // 8, eight, 0)

    def keep(o, row):
        rows = pl.ds(pl.multiple_of(row, block), block)
        for i in range(wide):
            high, low = split(x_ref[i, o * block : (o + 1) * block])
            out_ref[0, o % pairs, rows, columns(i)] = high
            out_ref[1, o % pairs, rows, columns(i)] = low

    for o in range(pairs):
        keep(o, base)

    @pl.when(base * 2 >= degrees)
    def _():
        for o in range(pairs, 2 * pairs):
            keep(o, base + degrees // 2)


def legendre_table(orders, lat_count, degrees):
    colatitude = np.pi * (np.arange(lat_count) + 0.5) / lat_count
    sine = np.sin(colatitude)
    trig = np.stack(
        [np.cos(colatitude), np.log(sine), math.sqrt(np.pi / lat_count) * sine]
    ).astype(np.float32)
    ladder = np.arange(1, degrees)
    logs = 0.5 * math.log(0.5) + np.concatenate(
        [[0.0], np.cumsum(0.5 * np.log((2.0 * ladder + 1.0) / (2.0 * ladder)))]
    )
    level = np.arange(degrees, dtype=np.float64)
    inverse = (1.0 / np.maximum(4.0 * level * level - 1.0, 1.0)).astype(np.float32)
    start = jnp.take(jnp.asarray(logs, jnp.float32), orders)[:, None]
    block = 64
    shape = (2, 4, degrees * 3 // 2, lat_count)
    vmem = pl.BlockSpec(memory_space=pltpu.VMEM)
    return pl.pallas_call(
        legendre_kernel,
        grid=(degrees // block,),
        in_specs=[pl.BlockSpec(memory_space=pltpu.SMEM), vmem, vmem, vmem],
        out_specs=pl.BlockSpec(shape, lambda i: (0, 0, 0, 0)),
        out_shape=jax.ShapeDtypeStruct(shape, jnp.bfloat16),
        scratch_shapes=[pltpu.VMEM((8, lat_count), jnp.float32)] * 4
        + [pltpu.VMEM((lat_count // LANES, 8 * block, LANES), jnp.float32)],
        name="legendre_table",
    )(inverse, orders.astype(jnp.float32)[:, None], start, trig)


def project_kernel(begin, m_ref, o_ref, rad_ref, z_ref, t_ref, e_ref, *refs):
    *out_refs, tile_ref, eig_ref, s_ref, q_ref, sem = refs
    lat_count = tile_ref.shape[-1]
    block = LANES
    shells, modes, degrees = e_ref.shape
    quarter = modes // 4
    pairs = q_ref.shape[1]
    copies = [
        pltpu.make_async_copy(t_ref.at[:, begin + pair], tile_ref.at[pair], sem.at[pair])
        for pair in range(pairs)
    ]
    eigen_copy = pltpu.make_async_copy(e_ref, eig_ref, sem.at[pairs])
    copies[0].start()
    eigen_copy.start()
    for copy in copies[1:]:
        copy.start()
    degree = lax.broadcasted_iota(jnp.int32, (degrees, LANES), 0).astype(jnp.float32)
    factor = degree * (degree + 1.0)

    for pair in range(pairs):
        copies[pair].wait()
        found = []
        for which, (first, count) in enumerate(((0, degrees), (degrees // 2, degrees // 2))):
            o = o_ref[which, begin + pair]
            data = jnp.concatenate(split(z_ref[pl.ds(o, lat_count, stride=8), :]), axis=1)
            rows = slice(which * degrees, which * degrees + count)
            table = jnp.concatenate([tile_ref[pair, 0, rows], tile_ref[pair, 1, rows]], axis=0)
            parts = jnp.dot(table, data, preferred_element_type=jnp.float32)
            both = parts[:count, :LANES] + (parts[:count, LANES:] + parts[count:, :LANES])
            source = both - factor[first : first + count] * pltpu.roll(both, LANES // 2, 1)
            for b in range(count // block):
                s_ref[len(found) + b] = source[b * block : (b + 1) * block].T
            found += [first + b * block for b in range(count // block)]
        if pair == 0:
            eigen_copy.wait()
        kept = []
        for i, first in enumerate(found):
            totals = [jnp.zeros((modes, block), jnp.float32) for _ in range(2)]
            for r in range(shells):
                eigen = eig_ref[r, :, first : first + block]
                for part in range(2):
                    row = part * shells + r
                    totals[part] = totals[part] + eigen * s_ref[i, row : row + 1, :]
            kept.append(totals)
        low_blocks = degrees // block
        wide_pair = m_ref[begin + pair] < block
        places = [
            [jnp.where(wide_pair, x, y) for x, y in zip(kept[0], kept[low_blocks])]
        ] + kept[1:low_blocks] + kept[low_blocks + 1 :]
        for place, totals in enumerate(places):
            for part in range(2):
                for q in range(4):
                    q_ref[q, pair, place, part] = totals[part][q * quarter : (q + 1) * quarter]

    for relative, out_ref in enumerate(out_refs):
        out_ref[...] = q_ref[rad_ref[0] ^ relative]


def projected(begin, pairs, lower, places, rad, spectrum, table, eigen):
    lat_count = table.shape[-1]
    shells, modes, degrees = eigen.shape
    block = LANES
    smem = pl.BlockSpec(memory_space=pltpu.SMEM)
    vmem = pl.BlockSpec(memory_space=pltpu.VMEM)
    hbm = pl.BlockSpec(memory_space=pl.ANY)
    shape = (pairs, degrees // block + 1, 2, modes // 4, block)
    return pl.pallas_call(
        functools.partial(project_kernel, begin),
        in_specs=[smem, smem, smem, vmem, hbm, hbm],
        out_specs=[vmem] * 4,
        out_shape=[jax.ShapeDtypeStruct(shape, jnp.float32)] * 4,
        scratch_shapes=[
            pltpu.VMEM((pairs, 2) + table.shape[2:], jnp.bfloat16),
            pltpu.VMEM(eigen.shape, jnp.float32),
            pltpu.VMEM((degrees * 3 // 2 // block, LANES, block), jnp.float32),
            pltpu.VMEM((4,) + shape, jnp.float32),
            pltpu.SemaphoreType.DMA((pairs + 1,)),
        ],
        name="project",
    )(lower, places, rad, spectrum.reshape(lat_count * 8, LANES), table, eigen)


def finish_kernel(m_ref, slot_ref, *refs):
    *in_refs, out_ref = refs
    groups = len(in_refs) // 4
    pairs, places = in_refs[0].shape[:2]
    block = in_refs[0].shape[-1]
    for group in range(groups):
        mine = in_refs[group * 4 : group * 4 + 4]
        for pair in range(pairs):
            at = group * pairs + pair
            wide_pair = m_ref[at] < block
            low, high = slot_ref[0, at], slot_ref[1, at]

            def total(place):
                return (mine[0][pair, place] + mine[1][pair, place]) + (
                    mine[2][pair, place] + mine[3][pair, place]
                )

            first = total(0)
            zero = jnp.zeros_like(first)
            out_ref[low, :, :, 0:block] = jnp.where(wide_pair, first, zero)
            for place in range(1, places - 1):
                out_ref[low, :, :, place * block : (place + 1) * block] = total(place)
            for place in range(places - 3):
                out_ref[high, :, :, place * block : (place + 1) * block] = zero
            out_ref[high, :, :, (places - 3) * block : (places - 2) * block] = jnp.where(
                wide_pair, zero, first
            )
            out_ref[high, :, :, (places - 2) * block :] = total(places - 1)


def finished(lower, slots, parts):
    pairs, places, kinds, modes, block = parts[0].shape
    count = 2 * pairs * (len(parts) // 4)
    smem = pl.BlockSpec(memory_space=pltpu.SMEM)
    vmem = pl.BlockSpec(memory_space=pltpu.VMEM)
    return pl.pallas_call(
        finish_kernel,
        in_specs=[smem, smem] + [vmem] * len(parts),
        out_specs=vmem,
        out_shape=jax.ShapeDtypeStruct((count, kinds, modes, (places - 1) * block), jnp.float32),
        name="finish",
    )(lower, slots, *parts)


def body(velocity, density, offsets, radial_weights, angular_scale, order_table, eigenfunctions):
    lats, lon = velocity.shape[2:]
    velocity = jnp.transpose(velocity, (0, 2, 1, 3))
    degrees = order_table.shape[0]
    groups = lax.axis_size("lat")
    size = lax.axis_size("rad")
    lat_count = lats * groups
    where = lax.axis_index("lat")

    top, bottom = halo_cross(density, velocity)
    up = [(i, i + 1) for i in range(size - 1)]
    below = lax.ppermute(top, "rad", up)
    above = lax.ppermute(bottom, "rad", [(j, i) for i, j in up])
    pairs = order_table.reshape(degrees // 2, 2)
    tables = gathered_tables(pairs[:, 0][None, :], master_tables(lon, degrees))
    by_slot = fourier(
        offsets, density, radial_weights, angular_scale, velocity, below, above, tables
    )
    by_slot = by_slot.reshape(groups, lats, 8, LANES)
    gathered = lax.all_to_all(by_slot, "lat", split_axis=0, concat_axis=0, tiled=True)
    gathered = gathered.reshape(lat_count, 8, LANES)

    first = lax.dynamic_slice_in_dim(pairs, where * 4, 4)[:, 0]
    second = degrees - 1 - first
    first_half = (first & 1) == (where & 1)
    eigen = jnp.transpose(eigenfunctions, (2, 1, 0))
    first_low = first < degrees // 2
    lower = jnp.where(first_low, first, second)
    orders = jnp.concatenate([lower, degrees - 1 - lower])
    table = legendre_table(orders, lat_count, degrees)
    number = jnp.arange(4, dtype=jnp.int32)
    slot = 2 * number + jnp.where(first_low, 0, 1)
    slots = jnp.stack([slot, slot ^ 1])
    row = number + jnp.where(first_low == first_half, 0, 4)
    places = jnp.stack([row, row ^ 4])
    rad = lax.axis_index("rad")[None]
    parts = []
    for begin in (0, 2):
        own, *others = projected(
            begin, 2, lower, places, rad, gathered, table, eigen
        )
        parts.append(own)
        for relative, other in enumerate(others, 1):
            swap = [(i, i ^ relative) for i in range(size)]
            parts.append(lax.ppermute(other, "rad", swap))
    return finished(lower, slots, parts)


def solution(mesh):
    placed = (
        P(None, "rad", "lat", None),
        P("rad"),
        P(),
        P(None, None, "rad"),
        P("rad"),
        P(),
        P(None, None, "rad"),
    )
    return jax.shard_map(
        body, mesh=mesh, in_specs=placed, out_specs=P("lat", None, "rad", None), check_vma=False
    )
```

```python
import functools
import math

import jax
import jax.numpy as jnp
import numpy as np
from jax import lax
from jax.experimental import pallas as pl
from jax.experimental.pallas import tpu as pltpu
from jax.sharding import PartitionSpec as P


TAPS = 4
HALO = 3
LANES = 128
LEVEL = 60.0


def master_tables(lon, degrees):
    half = lon // 2
    orders = np.arange(degrees).reshape(degrees // 2, 2).T
    angle = (2.0 * np.pi / lon) * ((orders[:, :, None] * np.arange(half)) % lon)
    full = np.stack([np.cos(angle), -np.sin(angle)], axis=1) / math.sqrt(lon)
    high = full.astype(np.float32).astype(jnp.bfloat16)
    low = (full - high.astype(np.float64)).astype(np.float32).astype(jnp.bfloat16)
    return np.concatenate([high, low], axis=1)


def small(mebibytes=24):
    return pltpu.CompilerParams(vmem_limit_bytes=mebibytes * 2**20)


def split(x):
    high = x.astype(jnp.bfloat16)
    return high, (x - high.astype(jnp.float32)).astype(jnp.bfloat16)


def gather_kernel(first_ref, table_ref, out_ref):
    kinds, count = table_ref.shape[1:3]
    parity = pl.program_id(0)
    first = first_ref[...]
    even = jnp.where((first & 1) == 0, first, 2 * count - 1 - first)
    odd = 2 * count - 1 - even
    lane = lax.broadcasted_iota(jnp.int32, (1, count), 1)
    swapped = jnp.where((lane & 4) == 0, pltpu.roll(odd, count - 4, 1), pltpu.roll(odd, 4, 1))
    row = jnp.where(parity == 0, even, swapped) >> 1
    hot = (lax.broadcasted_iota(jnp.int32, (count, count), 0) == row).astype(jnp.float32)
    hot = hot.T.astype(jnp.bfloat16)
    for kind in range(kinds):
        out_ref[0, kind] = jnp.dot(
            hot, table_ref[0, kind], preferred_element_type=jnp.float32
        ).astype(jnp.bfloat16)


def gathered_tables(first, tables):
    block = pl.BlockSpec((1,) + tables.shape[1:], lambda p: (p, 0, 0, 0))
    return pl.pallas_call(
        gather_kernel,
        grid=(2,),
        in_specs=[pl.BlockSpec(memory_space=pltpu.VMEM), block],
        out_specs=block,
        out_shape=jax.ShapeDtypeStruct(tables.shape, jnp.bfloat16),
        compiler_params=small(),
        name="gather_rows",
    )(first, tables)


def halo_kernel(rho_ref, v_ref, top_ref, bottom_ref, flow_ref, sem):
    lats, shells, lon = v_ref.shape[1:]
    starts = (shells - 8, 0)
    copies = [
        [
            pltpu.make_async_copy(
                v_ref.at[k, :, pl.ds(start, 8)], flow_ref.at[i, k], sem.at[3 * i + k]
            )
            for k in range(3)
        ]
        for i, start in enumerate(starts)
    ]
    for side in copies:
        for copy in side:
            copy.start()
    wide = lon // LANES
    row = lax.broadcasted_iota(jnp.int32, (8, LANES), 0)
    for i, (start, out_ref) in enumerate(zip(starts, (top_ref, bottom_ref))):
        skip = 8 - HALO if i == 0 else 0
        rho = jnp.zeros((8, LANES), jnp.float32)
        for h in range(8):
            rho = jnp.where(row == h, rho_ref[start + h], rho)
        for copy in copies[i]:
            copy.wait()

        def band(lat, _, i=i, rho=rho, out_ref=out_ref, skip=skip):
            for c in range(wide):
                cols = slice(c * LANES, (c + 1) * LANES)
                radial, polar, azimuth = (
                    flow_ref[i, k, lat, :, cols].astype(jnp.float32) for k in range(3)
                )
                flux = rho * radial
                for k, value in enumerate((flux * polar, flux * azimuth)):
                    for h in range(HALO):
                        out_ref[k, h, pl.ds(lat * wide + c, 1)] = value[skip + h : skip + h + 1]
            return 0

        lax.fori_loop(0, lats, band, 0)


def halo_cross(density, velocity):
    _, lats, shells, lon = velocity.shape
    vmem = pl.BlockSpec(memory_space=pltpu.VMEM)
    shape = jax.ShapeDtypeStruct((2, HALO, lats * lon // LANES, LANES), jnp.float32)
    return pl.pallas_call(
        halo_kernel,
        in_specs=[pl.BlockSpec(memory_space=pltpu.SMEM), pl.BlockSpec(memory_space=pltpu.HBM)],
        out_specs=[vmem, vmem],
        out_shape=[shape, shape],
        scratch_shapes=[
            pltpu.VMEM((2, 3, lats, 8, lon), jnp.bfloat16),
            pltpu.SemaphoreType.DMA((6,)),
        ],
        compiler_params=small(),
        name="halo_cross",
    )(density, velocity)


CHUNK = 1


def chunk_copy(v_ref, flow_ref, sem, i):
    part = pl.ds(i * CHUNK, CHUNK)
    return pltpu.make_async_copy(v_ref.at[:, part], flow_ref.at[:, part], sem.at[i])


def start_chunks(v_ref, flow_ref, sem):
    for i in range(v_ref.shape[1] // CHUNK):
        chunk_copy(v_ref, flow_ref, sem, i).start()


def wait_chunk(v_ref, flow_ref, sem, lat):
    @pl.when(lat % CHUNK == 0)
    def _():
        chunk_copy(v_ref, flow_ref, sem, lat // CHUNK).wait()


def shell_rows(count, value):
    row = lax.broadcasted_iota(jnp.int32, (8, LANES), 0)
    tiles = []
    for base in range(0, count, 8):
        tile = jnp.zeros((8, LANES), jnp.float32)
        for h in range(8):
            tile = jnp.where(row == h, value(base + h), tile)
        tiles.append(tile)
    return jnp.concatenate(tiles, axis=0)


def store_folded(g_ref, lat, shells, chunk, a, b):
    place = (lat & ~3) + ((lat & 1) << 1) + ((lat & 2) >> 1)
    rows = pl.ds(pl.multiple_of(place * shells, shells), shells)
    cols = slice(chunk * LANES, (chunk + 1) * LANES)
    for parity, value in enumerate((a + b, a - b)):
        high, low = split(value)
        g_ref[parity, 0, rows, cols] = high
        g_ref[parity, 1, rows, cols] = low


def transform(g_ref, t_ref, shells, lats, emit):
    kinds, count, half = t_ref.shape[1:]
    nt = (((1,), (1,)), ((), ()))
    row = lax.broadcasted_iota(jnp.int32, (count, LANES), 0)
    lane = lax.broadcasted_iota(jnp.int32, (count, LANES), 1)
    upper = (row & 7) < 4
    straight = (lane & shells) == 0
    for start, size in ((0, 8), (8, 4)):
        rows = slice(start * shells, (start + size) * shells)
        sums = []
        for parity in range(2):
            table = t_ref[parity].reshape(kinds * count, half)
            high, low = g_ref[parity, 0, rows], g_ref[parity, 1, rows]
            if size == 8:
                main = lax.dot_general(table, high, nt, preferred_element_type=jnp.float32)
                rest = lax.dot_general(
                    table[: 2 * count], low, nt, preferred_element_type=jnp.float32
                )
                sums.append(main[: 2 * count] + main[2 * count :] + rest)
            else:
                both = jnp.concatenate([high, low], axis=0)
                main = lax.dot_general(table, both, nt, preferred_element_type=jnp.float32)
                width = size * shells
                sums.append(
                    main[: 2 * count, :width]
                    + (main[: 2 * count, width:] + main[2 * count :, :width])
                )
        for base in range(0, size, 4):
            cols = slice(base * shells, base * shells + LANES)
            found = []
            for total in sums:
                cosine, sine = total[:count, cols], total[count:, cols]
                found.append(
                    (
                        jnp.where(straight, cosine, pltpu.roll(sine, shells, 1)),
                        jnp.where(straight, pltpu.roll(cosine, LANES - shells, 1), sine),
                    )
                )
            for i in range(2):
                even, odd = found[0][i], found[1][i]
                tiles = (count // 8, 8, LANES)
                emit(
                    (start + base) // 2 + i,
                    jnp.where(upper, even, odd).reshape(tiles),
                    jnp.where(upper, odd, even).reshape(tiles),
                )


def angular_kernel(rho_ref, ang_ref, v_ref, t_ref, a_ref, flow_ref, g_ref, sem):
    lats, shells, lon = v_ref.shape[1:]
    wide = lon // LANES
    start_chunks(v_ref, flow_ref, sem)
    scale = shell_rows(shells, lambda r: ang_ref[r] * rho_ref[r])

    def band(lat, _):
        wait_chunk(v_ref, flow_ref, sem, lat)
        for chunk in range(wide // 2):
            terms = []
            for c in (chunk, chunk + wide // 2):
                cols = slice(c * LANES, (c + 1) * LANES)
                radial, polar, azimuth = (
                    flow_ref[k, lat, :, cols].astype(jnp.float32) for k in range(3)
                )
                terms.append(
                    scale
                    * (
                        polar * polar
                        + azimuth * azimuth
                        - 2.0 * radial * radial
                        + polar * azimuth
                    )
                )
            store_folded(g_ref, lat, shells, chunk, *terms)
        return 0

    lax.fori_loop(0, lats, band, 0)

    def emit(pair, left, right):
        a_ref[:, 0, pair] = left
        a_ref[:, 1, pair] = right

    transform(g_ref, t_ref, shells, lats, emit)


def radial_kernel(
    off_ref, rho_ref, w_ref, v_ref, lo_ref, hi_ref, t_ref, a_ref, out_ref, flow_ref, w_rows, c_ref, g_ref, y_ref, sem, out_sem
):
    lats, shells, lon = v_ref.shape[1:]
    wide = lon // LANES
    plane = lats * wide
    start_chunks(v_ref, flow_ref, sem)
    rho = shell_rows(shells, lambda r: rho_ref[r])
    for tap in range(TAPS):
        for k in range(2):
            w_rows[k, tap] = shell_rows(shells, lambda r: w_ref[k, tap, r])

    def band(lat, _):
        wait_chunk(v_ref, flow_ref, sem, lat)
        for c in range(wide):
            cols = slice(c * LANES, (c + 1) * LANES)
            radial, polar, azimuth = (
                flow_ref[k, lat, :, cols].astype(jnp.float32) for k in range(3)
            )
            flux = rho * radial
            c_ref[0, c, 8 : 8 + shells] = flux * polar
            c_ref[1, c, 8 : 8 + shells] = flux * azimuth
            for k in range(2):
                at = pl.ds(k * HALO * plane + lat * wide + c, HALO, stride=plane)
                c_ref[k, c, 8 - HALO : 8] = lo_ref[at, :]
                c_ref[k, c, 8 + shells : 8 + shells + HALO] = hi_ref[at, :]
        for chunk in range(wide // 2):
            terms = []
            for c in (chunk, chunk + wide // 2):
                total = jnp.zeros((shells, LANES), jnp.float32)
                for tap in range(TAPS):
                    at = pl.ds(8 + off_ref[tap], shells)
                    total = (
                        total
                        + w_rows[0, tap] * c_ref[0, c, at, :]
                        + w_rows[1, tap] * c_ref[1, c, at, :]
                    )
                terms.append(total)
            store_folded(g_ref, lat, shells, chunk, *terms)
        return 0

    lax.fori_loop(0, lats, band, 0)

    near = lax.broadcasted_iota(jnp.int32, y_ref.shape[:1] + (8, LANES), 2) < LANES // 2

    def emit(pair, *both):
        for i, mine in enumerate(both):
            other = a_ref[:, i, pair]
            y_ref[:, i, 2 * pair] = jnp.where(near, mine, pltpu.roll(other, LANES // 2, 2))
            y_ref[:, i, 2 * pair + 1] = jnp.where(near, pltpu.roll(mine, LANES // 2, 2), other)
        if pair % 2 == 1:
            out_copy(pair // 2).start()

    def out_copy(i):
        part = pl.ds(4 * i, 4)
        return pltpu.make_async_copy(y_ref.at[:, :, part], out_ref.at[:, :, part], out_sem.at[i])

    transform(g_ref, t_ref, shells, lats, emit)
    for i in range(lats // 4):
        out_copy(i).wait()


def fourier(offsets, density, weights, angular, velocity, below, above, tables):
    _, lats, shells, lon = velocity.shape
    count = tables.shape[2]
    smem = pl.BlockSpec(memory_space=pltpu.SMEM)
    vmem = pl.BlockSpec(memory_space=pltpu.VMEM)
    hbm = pl.BlockSpec(memory_space=pltpu.HBM)
    flow = pltpu.VMEM(velocity.shape, velocity.dtype)
    folded = pltpu.VMEM((2, 2, lats * shells, lon // 2), jnp.bfloat16)
    sems = pltpu.SemaphoreType.DMA((lats // CHUNK,))
    ready = pl.pallas_call(
        angular_kernel,
        in_specs=[smem, smem, hbm, vmem],
        out_specs=vmem,
        out_shape=jax.ShapeDtypeStruct((count // 8, 2, lats // 2, 8, LANES), jnp.float32),
        scratch_shapes=[flow, folded, sems],
        compiler_params=small(),
        name="angular",
    )(density, angular, velocity, tables)
    return pl.pallas_call(
        radial_kernel,
        in_specs=[smem] * 3 + [hbm] + [vmem] * 4,
        out_specs=hbm,
        out_shape=pltpu.HBM((count // 8, 2, lats, 8, LANES), jnp.float32),
        scratch_shapes=[
            flow,
            pltpu.VMEM((2, TAPS, shells, LANES), jnp.float32),
            pltpu.VMEM((2, lon // LANES, shells + 16, LANES), jnp.float32),
            folded,
            pltpu.VMEM((count // 8, 2, lats, 8, LANES), jnp.float32),
            sems,
            pltpu.SemaphoreType.DMA((lats // 4,)),
        ],
        compiler_params=small(),
        name="radial",
    )(
        offsets,
        density,
        weights,
        velocity,
        below.reshape(-1, LANES),
        above.reshape(-1, LANES),
        tables,
        ready,
    )


def legendre_kernel(inv_ref, m_ref, start_ref, trig_ref, out_ref, s_ref, p_ref, z_ref, e_ref, x_ref):
    block = x_ref.shape[1] // 8
    pairs = out_ref.shape[1]
    degrees = block * pl.num_programs(0)
    lat_count = trig_ref.shape[1]
    base = pl.program_id(0) * block
    wide = lat_count // LANES
    order = jnp.broadcast_to(m_ref[...], (8, LANES))
    quantum = LEVEL * math.log(2.0)

    def columns(i):
        return slice(i * LANES, (i + 1) * LANES)

    @pl.when(pl.program_id(0) == 0)
    def _():
        start = jnp.broadcast_to(start_ref[...], (8, LANES))
        for i in range(wide):
            log_value = start + order * trig_ref[1:2, columns(i)]
            level = jnp.minimum(jnp.ceil(log_value * (1.0 / quantum)), 0.0)
            z_ref[:, columns(i)] = (
                jnp.exp(log_value - level * quantum) * trig_ref[2:3, columns(i)]
            )
            e_ref[:, columns(i)] = level
        zero = jnp.zeros((8, lat_count), jnp.float32)
        s_ref[...] = zero
        p_ref[...] = zero

    def eight(chunk, _):
        levels, scales, current, older = [], [], [], []
        for i in range(wide):
            s = s_ref[:, columns(i)]
            p = p_ref[:, columns(i)]
            e = e_ref[:, columns(i)]
            grow = (jnp.maximum(jnp.abs(s), jnp.abs(p)) > 1.0) & (e < 0.0)
            shrink = jnp.where(grow, 2.0**-LEVEL, 1.0)
            e = e + jnp.where(grow, 1.0, 0.0)
            e_ref[:, columns(i)] = e
            current.append(s * shrink)
            older.append(p * shrink)
            scales.append(
                jnp.where(
                    e > -0.5,
                    1.0,
                    jnp.where(e > -1.5, 2.0**-LEVEL, jnp.where(e > -2.5, 2.0 ** (-2 * LEVEL), 0.0)),
                )
            )
        first = base + chunk * 8
        before = jnp.maximum(first - 1, 0)
        before_f = before.astype(jnp.float32)
        back = jnp.maximum((before_f * before_f - order * order) * inv_ref[before], 1e-7)
        back = jnp.sqrt(back)
        for step in range(8):
            degree = first + step
            level = degree.astype(jnp.float32)
            ratio = jnp.maximum((level * level - order * order) * inv_ref[degree], 1e-7)
            up = lax.rsqrt(ratio)
            up_back = up * back
            back = ratio * up
            starting = order == level
            for i in range(wide):
                entry = jnp.where(starting, z_ref[:, columns(i)], 0.0) - up_back * older[i]
                value = (up * trig_ref[0:1, columns(i)]) * current[i] + entry
                older[i] = current[i]
                current[i] = value
                x_ref[i, pl.ds(chunk * 8 + step, 8, stride=block), :] = value * scales[i]
        for i in range(wide):
            s_ref[:, columns(i)] = current[i]
            p_ref[:, columns(i)] = older[i]
        return 0

    lax.fori_loop(0, block // 8, eight, 0)

    def keep(o, row):
        rows = pl.ds(pl.multiple_of(row, block), block)
        for i in range(wide):
            high, low = split(x_ref[i, o * block : (o + 1) * block])
            out_ref[0, o % pairs, rows, columns(i)] = high
            out_ref[1, o % pairs, rows, columns(i)] = low

    for o in range(pairs):
        keep(o, base)

    @pl.when(base * 2 >= degrees)
    def _():
        for o in range(pairs, 2 * pairs):
            keep(o, base + degrees // 2)


def legendre_table(orders, lat_count, degrees):
    colatitude = np.pi * (np.arange(lat_count) + 0.5) / lat_count
    sine = np.sin(colatitude)
    trig = np.stack(
        [np.cos(colatitude), np.log(sine), math.sqrt(np.pi / lat_count) * sine]
    ).astype(np.float32)
    ladder = np.arange(1, degrees)
    logs = 0.5 * math.log(0.5) + np.concatenate(
        [[0.0], np.cumsum(0.5 * np.log((2.0 * ladder + 1.0) / (2.0 * ladder)))]
    )
    level = np.arange(degrees, dtype=np.float64)
    inverse = (1.0 / np.maximum(4.0 * level * level - 1.0, 1.0)).astype(np.float32)
    start = jnp.take(jnp.asarray(logs, jnp.float32), orders)[:, None]
    block = 64
    shape = (2, 4, degrees * 3 // 2, lat_count)
    vmem = pl.BlockSpec(memory_space=pltpu.VMEM)
    return pl.pallas_call(
        legendre_kernel,
        grid=(degrees // block,),
        in_specs=[pl.BlockSpec(memory_space=pltpu.SMEM), vmem, vmem, vmem],
        out_specs=pl.BlockSpec(shape, lambda i: (0, 0, 0, 0)),
        out_shape=jax.ShapeDtypeStruct(shape, jnp.bfloat16),
        scratch_shapes=[pltpu.VMEM((8, lat_count), jnp.float32)] * 4
        + [pltpu.VMEM((lat_count // LANES, 8 * block, LANES), jnp.float32)],
        compiler_params=small(),
        name="legendre_table",
    )(inverse, orders.astype(jnp.float32)[:, None], start, trig)


def project_kernel(begin, m_ref, o_ref, rad_ref, z_ref, t_ref, e_ref, *refs):
    *out_refs, tile_ref, eig_ref, s_ref, q_ref, sem = refs
    lat_count = tile_ref.shape[-1]
    block = LANES
    shells, modes, degrees = e_ref.shape
    quarter = modes // 4
    pairs = q_ref.shape[1]
    step = degrees // 2
    copies = [
        [
            pltpu.make_async_copy(
                t_ref.at[kind, begin + pair, pl.ds(first, step)],
                tile_ref.at[pair, kind, pl.ds(first, step)],
                sem.at[6 * pair + 3 * kind + first // step],
            )
            for first in rows
            for kind in range(2)
        ]
        for pair in range(pairs)
        for rows in ((0, step), (degrees,))
    ]
    share = shells // 4
    eigen_copies = [
        pltpu.make_async_copy(
            e_ref.at[pl.ds(i * share, share)],
            eig_ref.at[pl.ds(i * share, share)],
            sem.at[6 * pairs + i],
        )
        for i in range(4)
    ]
    for batch in copies[:2] + [eigen_copies] + copies[2:]:
        for copy in batch:
            copy.start()
    degree = lax.broadcasted_iota(jnp.int32, (degrees, LANES), 0).astype(jnp.float32)
    factor = degree * (degree + 1.0)

    for pair in range(pairs):
        found = []
        for which, (first, count) in enumerate(((0, degrees), (degrees // 2, degrees // 2))):
            o = o_ref[which, begin + pair]
            for copy in copies[2 * pair + which]:
                copy.wait()
            data = jnp.concatenate(split(z_ref[pl.ds(o, lat_count, stride=8), :]), axis=1)
            rows = slice(which * degrees, which * degrees + count)
            table = jnp.concatenate([tile_ref[pair, 0, rows], tile_ref[pair, 1, rows]], axis=0)
            parts = jnp.dot(table, data, preferred_element_type=jnp.float32)
            both = parts[:count, :LANES] + (parts[:count, LANES:] + parts[count:, :LANES])
            source = both - factor[first : first + count] * pltpu.roll(both, LANES // 2, 1)
            for b in range(count // block):
                s_ref[len(found) + b] = source[b * block : (b + 1) * block].T
            found += [first + b * block for b in range(count // block)]
        if pair == 0:
            for copy in eigen_copies:
                copy.wait()
        kept = []
        for i, first in enumerate(found):
            totals = [jnp.zeros((modes, block), jnp.float32) for _ in range(2)]
            for r in range(shells):
                eigen = eig_ref[r, :, first : first + block]
                for part in range(2):
                    row = part * shells + r
                    totals[part] = totals[part] + eigen * s_ref[i, row : row + 1, :]
            kept.append(totals)
        low_blocks = degrees // block
        wide_pair = m_ref[begin + pair] < block
        places = [
            [jnp.where(wide_pair, x, y) for x, y in zip(kept[0], kept[low_blocks])]
        ] + kept[1:low_blocks] + kept[low_blocks + 1 :]
        for place, totals in enumerate(places):
            for part in range(2):
                for q in range(4):
                    q_ref[q, pair, place, part] = totals[part][q * quarter : (q + 1) * quarter]

    for relative, out_ref in enumerate(out_refs):
        out_ref[...] = q_ref[rad_ref[0] ^ relative]


def projected(begin, pairs, lower, places, rad, spectrum, table, eigen):
    lat_count = table.shape[-1]
    shells, modes, degrees = eigen.shape
    block = LANES
    smem = pl.BlockSpec(memory_space=pltpu.SMEM)
    vmem = pl.BlockSpec(memory_space=pltpu.VMEM)
    hbm = pl.BlockSpec(memory_space=pltpu.HBM)
    shape = (pairs, degrees // block + 1, 2, modes // 4, block)
    return pl.pallas_call(
        functools.partial(project_kernel, begin),
        in_specs=[smem, smem, smem, vmem, hbm, hbm],
        out_specs=[vmem] * 4,
        out_shape=[jax.ShapeDtypeStruct(shape, jnp.float32)] * 4,
        scratch_shapes=[
            pltpu.VMEM((pairs, 2) + table.shape[2:], jnp.bfloat16),
            pltpu.VMEM(eigen.shape, jnp.float32),
            pltpu.VMEM((degrees * 3 // 2 // block, LANES, block), jnp.float32),
            pltpu.VMEM((4,) + shape, jnp.float32),
            pltpu.SemaphoreType.DMA((6 * pairs + 4,)),
        ],
        compiler_params=small(36),
        name="project",
    )(lower, places, rad, spectrum.reshape(lat_count * 8, LANES), table, eigen)


def finish_kernel(m_ref, slot_ref, *refs):
    *in_refs, out_ref = refs
    groups = len(in_refs) // 4
    pairs, places = in_refs[0].shape[:2]
    block = in_refs[0].shape[-1]
    for group in range(groups):
        mine = in_refs[group * 4 : group * 4 + 4]
        for pair in range(pairs):
            at = group * pairs + pair
            wide_pair = m_ref[at] < block
            low, high = slot_ref[0, at], slot_ref[1, at]

            def total(place):
                return (mine[0][pair, place] + mine[1][pair, place]) + (
                    mine[2][pair, place] + mine[3][pair, place]
                )

            first = total(0)
            zero = jnp.zeros_like(first)
            out_ref[low, :, :, 0:block] = jnp.where(wide_pair, first, zero)
            for place in range(1, places - 1):
                out_ref[low, :, :, place * block : (place + 1) * block] = total(place)
            for place in range(places - 3):
                out_ref[high, :, :, place * block : (place + 1) * block] = zero
            out_ref[high, :, :, (places - 3) * block : (places - 2) * block] = jnp.where(
                wide_pair, zero, first
            )
            out_ref[high, :, :, (places - 2) * block :] = total(places - 1)


def finished(lower, slots, parts):
    pairs, places, kinds, modes, block = parts[0].shape
    count = 2 * pairs * (len(parts) // 4)
    smem = pl.BlockSpec(memory_space=pltpu.SMEM)
    vmem = pl.BlockSpec(memory_space=pltpu.VMEM)
    return pl.pallas_call(
        finish_kernel,
        in_specs=[smem, smem] + [vmem] * len(parts),
        out_specs=vmem,
        out_shape=jax.ShapeDtypeStruct((count, kinds, modes, (places - 1) * block), jnp.float32),
        compiler_params=small(),
        name="finish",
    )(lower, slots, *parts)


def body(velocity, density, offsets, radial_weights, angular_scale, order_table, eigenfunctions):
    lats, lon = velocity.shape[2:]
    velocity = pltpu.with_memory_space_constraint(jnp.transpose(velocity, (0, 2, 1, 3)), pltpu.HBM)
    degrees = order_table.shape[0]
    groups = lax.axis_size("lat")
    size = lax.axis_size("rad")
    lat_count = lats * groups
    where = lax.axis_index("lat")

    top, bottom = halo_cross(density, velocity)
    up = [(i, i + 1) for i in range(size - 1)]
    below = lax.ppermute(top, "rad", up)
    above = lax.ppermute(bottom, "rad", [(j, i) for i, j in up])
    pairs = order_table.reshape(degrees // 2, 2)
    tables = gathered_tables(pairs[:, 0][None, :], master_tables(lon, degrees))
    by_slot = fourier(
        offsets, density, radial_weights, angular_scale, velocity, below, above, tables
    )
    by_slot = by_slot.reshape(groups, lats, 8, LANES)
    gathered = lax.all_to_all(by_slot, "lat", split_axis=0, concat_axis=0, tiled=True)
    gathered = gathered.reshape(lat_count, 8, LANES)

    first = lax.dynamic_slice_in_dim(pairs, where * 4, 4)[:, 0]
    second = degrees - 1 - first
    first_half = (first & 1) == (where & 1)
    eigen = jnp.transpose(eigenfunctions, (2, 1, 0))
    first_low = first < degrees // 2
    lower = jnp.where(first_low, first, second)
    orders = jnp.concatenate([lower, degrees - 1 - lower])
    table = legendre_table(orders, lat_count, degrees)
    number = jnp.arange(4, dtype=jnp.int32)
    slot = 2 * number + jnp.where(first_low, 0, 1)
    slots = jnp.stack([slot, slot ^ 1])
    row = number + jnp.where(first_low == first_half, 0, 4)
    places = jnp.stack([row, row ^ 4])
    rad = lax.axis_index("rad")[None]
    table, eigen = (pltpu.with_memory_space_constraint(x, pltpu.HBM) for x in (table, eigen))
    parts = []
    for begin in (0,):
        own, *others = projected(
            begin, 4, lower, places, rad, gathered, table, eigen
        )
        parts.append(own)
        for relative, other in enumerate(others, 1):
            swap = [(i, i ^ relative) for i in range(size)]
            parts.append(lax.ppermute(other, "rad", swap))
    return finished(lower, slots, parts)


def solution(mesh):
    placed = (
        P(None, "rad", "lat", None),
        P("rad"),
        P(),
        P(None, None, "rad"),
        P("rad"),
        P(),
        P(None, None, "rad"),
    )
    return jax.shard_map(
        body, mesh=mesh, in_specs=placed, out_specs=P("lat", None, "rad", None), check_vma=False
    )
```

```python
import math

import jax
import jax.numpy as jnp
import numpy as np
from jax import lax
from jax.experimental import pallas as pl
from jax.experimental.pallas import tpu as pltpu
from jax.sharding import PartitionSpec as P


TAPS = 4
HALO = 3
LANES = 128
LAT_SPLIT = ("x", "z2", "z1", "z0", "y1", "y0")
SENT = ("y0", "y1", "x", "z0", "z1", "z2")
LEVEL = 60.0


def master_tables(lon, degrees):
    half = lon // 2
    orders = np.arange(degrees).reshape(degrees // 2, 2).T
    angle = (2.0 * np.pi / lon) * ((orders[:, :, None] * np.arange(half)) % lon)
    full = np.stack([np.cos(angle), -np.sin(angle)], axis=1) / math.sqrt(lon)
    high = full.astype(np.float32).astype(jnp.bfloat16)
    low = (full - high.astype(np.float64)).astype(np.float32).astype(jnp.bfloat16)
    return np.concatenate([high, low], axis=1)


def small(mebibytes=24):
    return pltpu.CompilerParams(vmem_limit_bytes=mebibytes * 2**20)


def split(x):
    high = x.astype(jnp.bfloat16)
    return high, (x - high.astype(jnp.float32)).astype(jnp.bfloat16)


def gather_kernel(first_ref, table_ref, out_ref):
    kinds, count = table_ref.shape[1:3]
    parity = pl.program_id(0)
    first = first_ref[...]
    even = jnp.where((first & 1) == 0, first, 2 * count - 1 - first)
    odd = 2 * count - 1 - even
    lane = lax.broadcasted_iota(jnp.int32, (1, count), 1)
    swapped = jnp.where((lane & 4) == 0, pltpu.roll(odd, count - 4, 1), pltpu.roll(odd, 4, 1))
    row = jnp.where(parity == 0, even, swapped) >> 1
    hot = (lax.broadcasted_iota(jnp.int32, (count, count), 0) == row).astype(jnp.float32)
    hot = hot.T.astype(jnp.bfloat16)
    for kind in range(kinds):
        out_ref[0, kind] = jnp.dot(
            hot, table_ref[0, kind], preferred_element_type=jnp.float32
        ).astype(jnp.bfloat16)


def gathered_tables(first, tables):
    block = pl.BlockSpec((1,) + tables.shape[1:], lambda p: (p, 0, 0, 0))
    return pl.pallas_call(
        gather_kernel,
        grid=(2,),
        in_specs=[pl.BlockSpec(memory_space=pltpu.VMEM), block],
        out_specs=block,
        out_shape=jax.ShapeDtypeStruct(tables.shape, jnp.bfloat16),
        compiler_params=small(),
        name="gather_rows",
    )(first, tables)


def halo_kernel(rho_ref, v_ref, top_ref, bottom_ref, flow_ref, sem):
    lats, shells, lon = v_ref.shape[1:]
    starts = (shells - 8, 0)
    copies = [
        [
            pltpu.make_async_copy(
                v_ref.at[k, :, pl.ds(start, 8)], flow_ref.at[i, k], sem.at[3 * i + k]
            )
            for k in range(3)
        ]
        for i, start in enumerate(starts)
    ]
    for side in copies:
        for copy in side:
            copy.start()
    wide = lon // LANES
    row = lax.broadcasted_iota(jnp.int32, (8, LANES), 0)
    for i, (start, out_ref) in enumerate(zip(starts, (top_ref, bottom_ref))):
        skip = 8 - HALO if i == 0 else 0
        rho = jnp.zeros((8, LANES), jnp.float32)
        for h in range(8):
            rho = jnp.where(row == h, rho_ref[start + h], rho)
        for copy in copies[i]:
            copy.wait()

        def band(lat, _, i=i, rho=rho, out_ref=out_ref, skip=skip):
            for c in range(wide):
                cols = slice(c * LANES, (c + 1) * LANES)
                radial, polar, azimuth = (
                    flow_ref[i, k, lat, :, cols].astype(jnp.float32) for k in range(3)
                )
                flux = rho * radial
                for k, value in enumerate((flux * polar, flux * azimuth)):
                    for h in range(HALO):
                        out_ref[k, h, pl.ds(lat * wide + c, 1)] = value[skip + h : skip + h + 1]
            return 0

        lax.fori_loop(0, lats, band, 0)


def halo_cross(density, velocity):
    _, lats, shells, lon = velocity.shape
    vmem = pl.BlockSpec(memory_space=pltpu.VMEM)
    shape = jax.ShapeDtypeStruct((2, HALO, lats * lon // LANES, LANES), jnp.float32)
    return pl.pallas_call(
        halo_kernel,
        in_specs=[pl.BlockSpec(memory_space=pltpu.SMEM), pl.BlockSpec(memory_space=pltpu.HBM)],
        out_specs=[vmem, vmem],
        out_shape=[shape, shape],
        scratch_shapes=[
            pltpu.VMEM((2, 3, lats, 8, lon), jnp.bfloat16),
            pltpu.SemaphoreType.DMA((6,)),
        ],
        compiler_params=small(),
        name="halo_cross",
    )(density, velocity)


def shell_rows(count, value):
    row = lax.broadcasted_iota(jnp.int32, (8, LANES), 0)
    tiles = []
    for base in range(0, count, 8):
        tile = jnp.zeros((8, LANES), jnp.float32)
        for h in range(8):
            tile = jnp.where(row == h, value(base + h), tile)
        tiles.append(tile)
    return jnp.concatenate(tiles, axis=0)


def store_folded(g_ref, lat, shells, chunk, a, b):
    place = (lat & ~3) + ((lat & 1) << 1) + ((lat & 2) >> 1)
    rows = pl.ds(pl.multiple_of(place * shells, shells), shells)
    cols = slice(chunk * LANES, (chunk + 1) * LANES)
    for parity, value in enumerate((a + b, a - b)):
        high, low = split(value)
        g_ref[parity, 0, rows, cols] = high
        g_ref[parity, 1, rows, cols] = low


def transform(g_ref, t_ref, shells, lats, emit):
    kinds, count, half = t_ref.shape[1:]
    nt = (((1,), (1,)), ((), ()))
    row = lax.broadcasted_iota(jnp.int32, (count, LANES), 0)
    lane = lax.broadcasted_iota(jnp.int32, (count, LANES), 1)
    upper = (row & 7) < 4
    straight = (lane & shells) == 0
    for start, size in ((0, 8), (8, 4)):
        rows = slice(start * shells, (start + size) * shells)
        sums = []
        for parity in range(2):
            table = t_ref[parity].reshape(kinds * count, half)
            high, low = g_ref[parity, 0, rows], g_ref[parity, 1, rows]
            if size == 8:
                main = lax.dot_general(table, high, nt, preferred_element_type=jnp.float32)
                rest = lax.dot_general(
                    table[: 2 * count], low, nt, preferred_element_type=jnp.float32
                )
                sums.append(main[: 2 * count] + main[2 * count :] + rest)
            else:
                both = jnp.concatenate([high, low], axis=0)
                main = lax.dot_general(table, both, nt, preferred_element_type=jnp.float32)
                width = size * shells
                sums.append(
                    main[: 2 * count, :width]
                    + (main[: 2 * count, width:] + main[2 * count :, :width])
                )
        for base in range(0, size, 4):
            cols = slice(base * shells, base * shells + LANES)
            found = []
            for total in sums:
                cosine, sine = total[:count, cols], total[count:, cols]
                found.append(
                    (
                        jnp.where(straight, cosine, pltpu.roll(sine, shells, 1)),
                        jnp.where(straight, pltpu.roll(cosine, LANES - shells, 1), sine),
                    )
                )
            for i in range(2):
                even, odd = found[0][i], found[1][i]
                tiles = (count // 8, 8, LANES)
                emit(
                    (start + base) // 2 + i,
                    jnp.where(upper, even, odd).reshape(tiles),
                    jnp.where(upper, odd, even).reshape(tiles),
                )


def angular_kernel(rho_ref, ang_ref, v_ref, t_ref, a_ref, g_ref):
    lats, shells, lon = v_ref.shape[1:]
    wide = lon // LANES
    scale = shell_rows(shells, lambda r: ang_ref[r] * rho_ref[r])

    def band(lat, _):
        for chunk in range(wide // 2):
            terms = []
            for c in (chunk, chunk + wide // 2):
                cols = slice(c * LANES, (c + 1) * LANES)
                radial, polar, azimuth = (
                    v_ref[k, lat, :, cols].astype(jnp.float32) for k in range(3)
                )
                terms.append(
                    scale
                    * (
                        polar * polar
                        + azimuth * azimuth
                        - 2.0 * radial * radial
                        + polar * azimuth
                    )
                )
            store_folded(g_ref, lat, shells, chunk, *terms)
        return 0

    lax.fori_loop(0, lats, band, 0)

    def emit(pair, left, right):
        a_ref[:, 0, pair] = left
        a_ref[:, 1, pair] = right

    transform(g_ref, t_ref, shells, lats, emit)


def radial_kernel(
    off_ref, rho_ref, w_ref, v_ref, lo_ref, hi_ref, t_ref, a_ref, out_ref, w_rows, c_ref, g_ref, y_ref, out_sem
):
    lats, shells, lon = v_ref.shape[1:]
    wide = lon // LANES
    plane = lats * wide
    rho = shell_rows(shells, lambda r: rho_ref[r])
    for tap in range(TAPS):
        for k in range(2):
            w_rows[k, tap] = shell_rows(shells, lambda r: w_ref[k, tap, r])

    def band(lat, _):
        for c in range(wide):
            cols = slice(c * LANES, (c + 1) * LANES)
            radial, polar, azimuth = (
                v_ref[k, lat, :, cols].astype(jnp.float32) for k in range(3)
            )
            flux = rho * radial
            c_ref[0, c, 8 : 8 + shells] = flux * polar
            c_ref[1, c, 8 : 8 + shells] = flux * azimuth
            for k in range(2):
                at = pl.ds(k * HALO * plane + lat * wide + c, HALO, stride=plane)
                c_ref[k, c, 8 - HALO : 8] = lo_ref[at, :]
                c_ref[k, c, 8 + shells : 8 + shells + HALO] = hi_ref[at, :]
        for chunk in range(wide // 2):
            terms = []
            for c in (chunk, chunk + wide // 2):
                total = jnp.zeros((shells, LANES), jnp.float32)
                for tap in range(TAPS):
                    at = pl.ds(8 + off_ref[tap], shells)
                    total = (
                        total
                        + w_rows[0, tap] * c_ref[0, c, at, :]
                        + w_rows[1, tap] * c_ref[1, c, at, :]
                    )
                terms.append(total)
            store_folded(g_ref, lat, shells, chunk, *terms)
        return 0

    lax.fori_loop(0, lats, band, 0)

    near = lax.broadcasted_iota(jnp.int32, y_ref.shape[:1] + (8, LANES), 2) < LANES // 2

    def emit(pair, *both):
        for i, mine in enumerate(both):
            other = a_ref[:, i, pair]
            y_ref[:, i, 2 * pair] = jnp.where(near, mine, pltpu.roll(other, LANES // 2, 2))
            y_ref[:, i, 2 * pair + 1] = jnp.where(near, pltpu.roll(mine, LANES // 2, 2), other)
        if pair % 2 == 1:
            out_copy(pair // 2).start()

    def out_copy(i):
        part = pl.ds(4 * i, 4)
        return pltpu.make_async_copy(y_ref.at[:, :, part], out_ref.at[:, :, part], out_sem.at[i])

    transform(g_ref, t_ref, shells, lats, emit)
    for i in range(lats // 4):
        out_copy(i).wait()


def fourier(offsets, density, weights, angular, velocity, below, above, tables):
    _, lats, shells, lon = velocity.shape
    count = tables.shape[2]
    smem = pl.BlockSpec(memory_space=pltpu.SMEM)
    vmem = pl.BlockSpec(memory_space=pltpu.VMEM)
    hbm = pl.BlockSpec(memory_space=pltpu.HBM)
    folded = pltpu.VMEM((2, 2, lats * shells, lon // 2), jnp.bfloat16)
    ready = pl.pallas_call(
        angular_kernel,
        in_specs=[smem, smem, vmem, vmem],
        out_specs=vmem,
        out_shape=jax.ShapeDtypeStruct((count // 8, 2, lats // 2, 8, LANES), jnp.float32),
        scratch_shapes=[folded],
        compiler_params=small(),
        name="angular",
    )(density, angular, velocity, tables)
    return pl.pallas_call(
        radial_kernel,
        in_specs=[smem] * 3 + [vmem] * 5,
        out_specs=hbm,
        out_shape=pltpu.HBM((count // 8, 2, lats, 8, LANES), jnp.float32),
        scratch_shapes=[
            pltpu.VMEM((2, TAPS, shells, LANES), jnp.float32),
            pltpu.VMEM((2, lon // LANES, shells + 16, LANES), jnp.float32),
            folded,
            pltpu.VMEM((count // 8, 2, lats, 8, LANES), jnp.float32),
            pltpu.SemaphoreType.DMA((lats // 4,)),
        ],
        compiler_params=small(),
        name="radial",
    )(
        offsets,
        density,
        weights,
        velocity,
        below.reshape(-1, LANES),
        above.reshape(-1, LANES),
        tables,
        ready,
    )


def legendre_kernel(inv_ref, m_ref, start_ref, trig_ref, out_ref, s_ref, p_ref, z_ref, e_ref, x_ref):
    block = x_ref.shape[1] // 8
    pairs = out_ref.shape[1]
    degrees = block * pl.num_programs(0)
    lat_count = trig_ref.shape[1]
    base = pl.program_id(0) * block
    wide = lat_count // LANES
    order = jnp.broadcast_to(m_ref[...], (8, LANES))
    quantum = LEVEL * math.log(2.0)

    def columns(i):
        return slice(i * LANES, (i + 1) * LANES)

    @pl.when(pl.program_id(0) == 0)
    def _():
        start = jnp.broadcast_to(start_ref[...], (8, LANES))
        for i in range(wide):
            log_value = start + order * trig_ref[1:2, columns(i)]
            level = jnp.minimum(jnp.ceil(log_value * (1.0 / quantum)), 0.0)
            z_ref[:, columns(i)] = (
                jnp.exp(log_value - level * quantum) * trig_ref[2:3, columns(i)]
            )
            e_ref[:, columns(i)] = level
        zero = jnp.zeros((8, lat_count), jnp.float32)
        s_ref[...] = zero
        p_ref[...] = zero

    def eight(chunk, _):
        levels, scales, current, older = [], [], [], []
        for i in range(wide):
            s = s_ref[:, columns(i)]
            p = p_ref[:, columns(i)]
            e = e_ref[:, columns(i)]
            grow = (jnp.maximum(jnp.abs(s), jnp.abs(p)) > 1.0) & (e < 0.0)
            shrink = jnp.where(grow, 2.0**-LEVEL, 1.0)
            e = e + jnp.where(grow, 1.0, 0.0)
            e_ref[:, columns(i)] = e
            current.append(s * shrink)
            older.append(p * shrink)
            scales.append(
                jnp.where(
                    e > -0.5,
                    1.0,
                    jnp.where(e > -1.5, 2.0**-LEVEL, jnp.where(e > -2.5, 2.0 ** (-2 * LEVEL), 0.0)),
                )
            )
        first = base + chunk * 8
        before = jnp.maximum(first - 1, 0)
        before_f = before.astype(jnp.float32)
        back = jnp.maximum((before_f * before_f - order * order) * inv_ref[before], 1e-7)
        back = jnp.sqrt(back)
        for step in range(8):
            degree = first + step
            level = degree.astype(jnp.float32)
            ratio = jnp.maximum((level * level - order * order) * inv_ref[degree], 1e-7)
            up = lax.rsqrt(ratio)
            up_back = up * back
            back = ratio * up
            starting = order == level
            for i in range(wide):
                entry = jnp.where(starting, z_ref[:, columns(i)], 0.0) - up_back * older[i]
                value = (up * trig_ref[0:1, columns(i)]) * current[i] + entry
                older[i] = current[i]
                current[i] = value
                x_ref[i, pl.ds(chunk * 8 + step, 8, stride=block), :] = value * scales[i]
        for i in range(wide):
            s_ref[:, columns(i)] = current[i]
            p_ref[:, columns(i)] = older[i]
        return 0

    lax.fori_loop(0, block // 8, eight, 0)

    def keep(o, row):
        rows = pl.ds(pl.multiple_of(row, block), block)
        for i in range(wide):
            high, low = split(x_ref[i, o * block : (o + 1) * block])
            out_ref[0, o % pairs, rows, columns(i)] = high
            out_ref[1, o % pairs, rows, columns(i)] = low

    for o in range(pairs):
        keep(o, base)

    @pl.when(base * 2 >= degrees)
    def _():
        for o in range(pairs, 2 * pairs):
            keep(o, base + degrees // 2)


def in_sent_order(x, dims):
    bits = len(LAT_SPLIT)
    split_bits = x.reshape((2,) * bits + (-1,) + dims)
    order = [LAT_SPLIT.index(name) for name in SENT]
    return split_bits.transpose(order + list(range(bits, split_bits.ndim)))


def legendre_table(orders, lat_count, degrees):
    colatitude = np.pi * (np.arange(lat_count) + 0.5) / lat_count
    colatitude = in_sent_order(colatitude, ()).reshape(-1)
    sine = np.sin(colatitude)
    trig = np.stack(
        [np.cos(colatitude), np.log(sine), math.sqrt(np.pi / lat_count) * sine]
    ).astype(np.float32)
    ladder = np.arange(1, degrees)
    logs = 0.5 * math.log(0.5) + np.concatenate(
        [[0.0], np.cumsum(0.5 * np.log((2.0 * ladder + 1.0) / (2.0 * ladder)))]
    )
    level = np.arange(degrees, dtype=np.float64)
    inverse = (1.0 / np.maximum(4.0 * level * level - 1.0, 1.0)).astype(np.float32)
    start = jnp.take(jnp.asarray(logs, jnp.float32), orders)[:, None]
    block = 64
    shape = (2, 4, degrees * 3 // 2, lat_count)
    vmem = pl.BlockSpec(memory_space=pltpu.VMEM)
    return pl.pallas_call(
        legendre_kernel,
        grid=(degrees // block,),
        in_specs=[pl.BlockSpec(memory_space=pltpu.SMEM), vmem, vmem, vmem],
        out_specs=pl.BlockSpec(shape, lambda i: (0, 0, 0, 0)),
        out_shape=jax.ShapeDtypeStruct(shape, jnp.bfloat16),
        scratch_shapes=[pltpu.VMEM((8, lat_count), jnp.float32)] * 4
        + [pltpu.VMEM((lat_count // LANES, 8 * block, LANES), jnp.float32)],
        compiler_params=small(),
        name="legendre_table",
    )(inverse, orders.astype(jnp.float32)[:, None], start, trig)


DEPTH = 4


def project_kernel(
    m_ref, o_ref, rad_ref, z_ref, t_ref, e_ref, own_ref, far_ref, send_ref, tile_ref, eig_ref, s_ref, q_ref, sem
):
    lat_count = tile_ref.shape[-1]
    block = LANES
    shells, modes, degrees = e_ref.shape
    quarter = modes // 4
    pairs = q_ref.shape[1]
    blocks = degrees // block

    def batch(pair, index, first, to, count):
        return [
            pltpu.make_async_copy(
                t_ref.at[kind, pair, pl.ds(first, count)],
                tile_ref.at[pair, kind, pl.ds(to, count)],
                sem.at[6 * pair + 3 * kind + index],
            )
            for kind in range(2)
        ]

    wide_pair = [m_ref[pair] < block for pair in range(pairs)]
    queue = []
    for pair in range(pairs):
        queue.append(batch(pair, 0, block, block, degrees - block))
        low = pl.multiple_of(jnp.where(wide_pair[pair], 0, degrees), block)
        queue.append(
            batch(pair, 1, low, 0, block)
            + batch(pair, 2, degrees * 3 // 2 - block, degrees, block)
        )
    share = shells // 4
    eigen_copies = [
        pltpu.make_async_copy(
            e_ref.at[pl.ds(i * share, share)],
            eig_ref.at[pl.ds(i * share, share)],
            sem.at[6 * pairs + i],
        )
        for i in range(4)
    ]
    queue.insert(4, eigen_copies)

    def start(i):
        for copy in queue[i] if i < len(queue) else ():
            copy.start()

    def wait(i):
        for copy in queue[i]:
            copy.wait()
        start(i + DEPTH)

    for i in range(DEPTH):
        start(i)
    degree = lax.broadcasted_iota(jnp.int32, (degrees, LANES), 0).astype(jnp.float32)
    factor = degree * (degree + 1.0)

    def sources(pair):
        low, high = (
            jnp.concatenate(split(z_ref[pl.ds(o_ref[i, pair], lat_count, stride=8), :]), axis=1)
            for i in range(2)
        )
        first = jnp.where(wide_pair[pair], factor[:block], factor[degrees // 2 : degrees // 2 + block])
        for part, (data, begin, count, scale) in enumerate(
            (
                (low, block, degrees - block, factor[block:]),
                (jnp.where(wide_pair[pair], low, high), 0, block, first),
                (high, degrees, block, factor[degrees - block :]),
            )
        ):
            number = 2 * pair + min(part, 1)
            if part < 2:
                wait(number if number < 4 else number + 1)
            rows = slice(begin, begin + count)
            main = jnp.dot(tile_ref[pair, 0, rows], data, preferred_element_type=jnp.float32)
            rest = jnp.dot(
                tile_ref[pair, 1, rows], data[:, :LANES], preferred_element_type=jnp.float32
            )
            both = main[:, :LANES] + (main[:, LANES:] + rest)
            source = both - scale * pltpu.roll(both, LANES // 2, 1)
            for i in range(count // block):
                s_ref[pair % 2, begin // block + i] = source[i * block : (i + 1) * block].T

    def modes_of(pair):
        start = pl.multiple_of(jnp.where(wide_pair[pair], 0, degrees // 2), block)
        for place in range(blocks + 1):
            first = start if place == 0 else min(place, blocks - 1) * block
            totals = [jnp.zeros((modes, block), jnp.float32) for _ in range(2)]
            for r in range(shells):
                eigen = eig_ref[r, :, pl.ds(first, block)]
                for part in range(2):
                    row = part * shells + r
                    totals[part] = totals[part] + eigen * s_ref[pair % 2, place, row : row + 1, :]
            for part in range(2):
                for q in range(4):
                    q_ref[q, pair, place, part] = totals[part][q * quarter : (q + 1) * quarter]

    sources(0)
    for pair in range(pairs):
        if pair + 1 < pairs:
            sources(pair + 1)
        if pair == 0:
            wait(4)
        modes_of(pair)
    own_ref[...] = q_ref[rad_ref[0]]
    far_ref[...] = q_ref[rad_ref[0] ^ 2]
    for i in range(2):
        send_ref[i] = q_ref[rad_ref[0] ^ (1 + 2 * i)]


def projected(lower, places, rad, spectrum, table, eigen):
    pairs = lower.shape[0]
    lat_count = table.shape[-1]
    shells, modes, degrees = eigen.shape
    block = LANES
    smem = pl.BlockSpec(memory_space=pltpu.SMEM)
    vmem = pl.BlockSpec(memory_space=pltpu.VMEM)
    hbm = pl.BlockSpec(memory_space=pltpu.HBM)
    shape = (pairs, degrees // block + 1, 2, modes // 4, block)
    return pl.pallas_call(
        project_kernel,
        in_specs=[smem, smem, smem, vmem, hbm, hbm],
        out_specs=[vmem] * 3,
        out_shape=[jax.ShapeDtypeStruct(x, jnp.float32) for x in (shape, shape, (2,) + shape)],
        scratch_shapes=[
            pltpu.VMEM((pairs, 2, degrees + block, lat_count), jnp.bfloat16),
            pltpu.VMEM(eigen.shape, jnp.float32),
            pltpu.VMEM((2, degrees // block + 1, LANES, block), jnp.float32),
            pltpu.VMEM((4,) + shape, jnp.float32),
            pltpu.SemaphoreType.DMA((6 * pairs + 4,)),
        ],
        compiler_params=small(36),
        name="project",
    )(lower, places, rad, spectrum.reshape(lat_count * 8, LANES), table, eigen)


def finish_kernel(m_ref, slot_ref, own_ref, near_ref, far_ref, out_ref):
    pairs, places = own_ref.shape[:2]
    block = own_ref.shape[-1]
    for pair in range(pairs):
        wide_pair = m_ref[pair] < block
        low, high = slot_ref[0, pair], slot_ref[1, pair]

        def total(place):
            return (own_ref[pair, place] + near_ref[0, pair, place]) + far_ref[pair, place]

        first = total(0)
        zero = jnp.zeros_like(first)
        out_ref[low, :, :, 0:block] = jnp.where(wide_pair, first, zero)
        for place in range(1, places - 1):
            out_ref[low, :, :, place * block : (place + 1) * block] = total(place)
        for place in range(places - 3):
            out_ref[high, :, :, place * block : (place + 1) * block] = zero
        out_ref[high, :, :, (places - 3) * block : (places - 2) * block] = jnp.where(
            wide_pair, zero, first
        )
        out_ref[high, :, :, (places - 2) * block :] = total(places - 1)


def finished(lower, slots, own, near, far):
    pairs, places, kinds, modes, block = own.shape
    smem = pl.BlockSpec(memory_space=pltpu.SMEM)
    vmem = pl.BlockSpec(memory_space=pltpu.VMEM)
    return pl.pallas_call(
        finish_kernel,
        in_specs=[smem, smem, vmem, vmem, vmem],
        out_specs=vmem,
        out_shape=jax.ShapeDtypeStruct(
            (2 * pairs, kinds, modes, (places - 1) * block), jnp.float32
        ),
        compiler_params=small(),
        name="finish",
    )(lower, slots, own, near, far)


def body(velocity, density, offsets, radial_weights, angular_scale, order_table, eigenfunctions):
    lats, lon = velocity.shape[2:]
    velocity = jnp.transpose(velocity, (0, 2, 1, 3))
    degrees = order_table.shape[0]
    groups = lax.axis_size(SENT)
    size = lax.axis_size("rad")
    lat_count = lats * groups
    where = lax.axis_index(LAT_SPLIT)
    place = lax.axis_index(SENT)

    top, bottom = halo_cross(density, pltpu.with_memory_space_constraint(velocity, pltpu.HBM))
    up = [(i, i + 1) for i in range(size - 1)]
    below = lax.ppermute(top, "rad", up)
    above = lax.ppermute(bottom, "rad", [(j, i) for i, j in up])
    pairs = order_table.reshape(degrees // 2, 2)
    by_group = in_sent_order(pairs[:, 0], ()).reshape(1, -1)
    tables = gathered_tables(by_group, master_tables(lon, degrees))
    by_slot = fourier(
        offsets, density, radial_weights, angular_scale, velocity, below, above, tables
    )
    by_slot = by_slot.reshape(groups, lats, 8, LANES)
    gathered = lax.all_to_all(by_slot, SENT, split_axis=0, concat_axis=0, tiled=True)
    gathered = gathered.reshape(lat_count, 8, LANES)

    first = lax.dynamic_slice_in_dim(pairs, where * 4, 4)[:, 0]
    second = degrees - 1 - first
    first_half = (first & 1) == (place & 1)
    eigen = jnp.transpose(eigenfunctions, (2, 1, 0))
    first_low = first < degrees // 2
    lower = jnp.where(first_low, first, second)
    orders = jnp.concatenate([lower, degrees - 1 - lower])
    table = legendre_table(orders, lat_count, degrees)
    number = jnp.arange(4, dtype=jnp.int32)
    slot = 2 * number + jnp.where(first_low, 0, 1)
    slots = jnp.stack([slot, slot ^ 1])
    row = number + jnp.where(first_low == first_half, 0, 4)
    places = jnp.stack([row, row ^ 4])
    rad = lax.axis_index("rad")[None]
    table, eigen = (pltpu.with_memory_space_constraint(x, pltpu.HBM) for x in (table, eigen))
    own, far, send = projected(lower, places, rad, gathered, table, eigen)
    near = lax.ppermute(send, "rad", [(i, i ^ 1) for i in range(size)])
    far = lax.ppermute(far + near[1], "rad", [(i, i ^ 2) for i in range(size)])
    return finished(lower, slots, own, near, far)


def solution(mesh):
    bits = len(LAT_SPLIT)
    mesh = jax.sharding.Mesh(
        mesh.devices.reshape((-1,) + (2,) * bits), ("rad",) + LAT_SPLIT
    )
    placed = (
        P(None, "rad", LAT_SPLIT, None),
        P("rad"),
        P(),
        P(None, None, "rad"),
        P("rad"),
        P(),
        P(None, None, "rad"),
    )
    return jax.shard_map(
        body, mesh=mesh, in_specs=placed, out_specs=P(LAT_SPLIT, None, "rad", None), check_vma=False
    )
```

```python
import math

import jax
import jax.numpy as jnp
import numpy as np
from jax import lax
from jax.experimental import pallas as pl
from jax.experimental.pallas import tpu as pltpu
from jax.sharding import PartitionSpec as P


TAPS = 4
HALO = 3
LANES = 128
LAT_SPLIT = ("x", "z2", "z1", "z0", "y1", "y0")
SENT = LAT_SPLIT
LEVEL = 60.0


def master_tables(lon, degrees):
    orders = np.arange(degrees).reshape(degrees // 2, 2).T[:, :, None]
    fine = (2.0 * np.pi / lon) * ((orders * np.arange(LANES)) % lon)
    coarse = (2.0 * np.pi / lon) * ((orders * LANES * np.arange(lon // 2 // LANES)) % lon)
    turns = np.concatenate([np.cos(coarse), np.sin(coarse)], axis=2)
    turns = np.pad(turns, ((0, 0), (0, 0), (0, LANES - turns.shape[2])))
    rest = np.concatenate(
        [np.cos(fine) / math.sqrt(lon), np.sin(fine) / math.sqrt(lon), turns], axis=2
    )
    terms = []
    for _ in range(3):
        terms.append(rest.astype(np.float32).astype(jnp.bfloat16))
        rest = rest - terms[-1].astype(np.float64)
    return np.concatenate(terms, axis=2)


def small(mebibytes=24):
    return pltpu.CompilerParams(vmem_limit_bytes=mebibytes * 2**20)


def split(x):
    high = x.astype(jnp.bfloat16)
    return high, (x - high.astype(jnp.float32)).astype(jnp.bfloat16)


def gather_kernel(first_ref, table_ref, out_ref):
    count = table_ref.shape[1]
    spot = lax.broadcasted_iota(jnp.int32, (1, LANES), 1)
    halves = []
    for base in range(0, count, LANES):
        half = jnp.zeros((1, LANES), jnp.int32)
        for i in range(LANES):
            half = jnp.where(spot == i, first_ref[2 * (base + i)], half)
        halves.append(half)
    first = jnp.concatenate(halves, axis=1)
    even = jnp.where((first & 1) == 0, first, 2 * count - 1 - first)
    odd = 2 * count - 1 - even
    lane = lax.broadcasted_iota(jnp.int32, (1, count), 1)
    swapped = jnp.where((lane & 4) == 0, pltpu.roll(odd, count - 4, 1), pltpu.roll(odd, 4, 1))
    wide = table_ref.shape[2] // 3
    steps = out_ref.shape[-1] // LANES
    for parity, orders in enumerate((even, swapped)):
        row = orders >> 1
        hot = (lax.broadcasted_iota(jnp.int32, (count, count), 0) == row).astype(jnp.float32)
        hot = hot.T.astype(jnp.bfloat16)
        terms = jnp.dot(hot, table_ref[parity], preferred_element_type=jnp.float32)
        found = terms[:, :wide] + (terms[:, wide : 2 * wide] + terms[:, 2 * wide :])
        cosine, sine, turns = (found[:, i * LANES : (i + 1) * LANES] for i in range(3))
        for a in range(steps):
            c, s = (
                jnp.broadcast_to(turns[:, i : i + 1], (count, LANES)) for i in (a, steps + a)
            )
            cols = slice(a * LANES, (a + 1) * LANES)
            for part, value in enumerate((c * cosine - s * sine, -(s * cosine + c * sine))):
                high, low = split(value)
                out_ref[parity, part, :, cols] = high
                out_ref[parity, 2 + part, :, cols] = low


def gathered_tables(first, tables, half):
    vmem = pl.BlockSpec(memory_space=pltpu.VMEM)
    return pl.pallas_call(
        gather_kernel,
        in_specs=[pl.BlockSpec(memory_space=pltpu.SMEM), vmem],
        out_specs=vmem,
        out_shape=jax.ShapeDtypeStruct((2, 4, tables.shape[1], half), jnp.bfloat16),
        compiler_params=small(),
        name="gather_rows",
    )(first, tables)


def halo_kernel(rho_ref, v_ref, top_ref, bottom_ref, flow_ref, sem):
    lats, shells, lon = v_ref.shape[1:]
    starts = (shells - 8, 0)
    copies = [
        [
            pltpu.make_async_copy(
                v_ref.at[k, :, pl.ds(start, 8)], flow_ref.at[i, k], sem.at[3 * i + k]
            )
            for k in range(3)
        ]
        for i, start in enumerate(starts)
    ]
    for side in copies:
        for copy in side:
            copy.start()
    wide = lon // LANES
    row = lax.broadcasted_iota(jnp.int32, (8, LANES), 0)
    for i, (start, out_ref) in enumerate(zip(starts, (top_ref, bottom_ref))):
        mine = row >= 8 - HALO if i == 0 else row < HALO
        away = 8 - HALO if i == 0 else HALO
        rho = jnp.zeros((8, LANES), jnp.float32)
        for h in range(8):
            rho = jnp.where(row == h, rho_ref[start + h], rho)
        for copy in copies[i]:
            copy.wait()

        def band(lat, _, i=i, rho=rho, out_ref=out_ref, mine=mine, away=away):
            for c in range(wide):
                cols = slice(c * LANES, (c + 1) * LANES)
                radial, polar, azimuth = (
                    flow_ref[i, k, lat, :, cols].astype(jnp.float32) for k in range(3)
                )
                flux = rho * radial
                other = pltpu.roll(flux * azimuth, away, 0)
                out_ref[lat * wide + c] = jnp.where(mine, flux * polar, other)
            return 0

        lax.fori_loop(0, lats, band, 0)


def halo_cross(density, velocity):
    _, lats, shells, lon = velocity.shape
    vmem = pl.BlockSpec(memory_space=pltpu.VMEM)
    shape = jax.ShapeDtypeStruct((lats * lon // LANES, 8, LANES), jnp.float32)
    return pl.pallas_call(
        halo_kernel,
        in_specs=[pl.BlockSpec(memory_space=pltpu.SMEM), pl.BlockSpec(memory_space=pltpu.HBM)],
        out_specs=[vmem, vmem],
        out_shape=[shape, shape],
        scratch_shapes=[
            pltpu.VMEM((2, 3, lats, 8, lon), jnp.bfloat16),
            pltpu.SemaphoreType.DMA((6,)),
        ],
        compiler_params=small(),
        name="halo_cross",
    )(density, velocity)


def shell_rows(count, value):
    row = lax.broadcasted_iota(jnp.int32, (8, LANES), 0)
    tiles = []
    for base in range(0, count, 8):
        tile = jnp.zeros((8, LANES), jnp.float32)
        for h in range(8):
            tile = jnp.where(row == h, value(base + h), tile)
        tiles.append(tile)
    return jnp.concatenate(tiles, axis=0)


def store_folded(g_ref, lat, shells, chunk, a, b):
    place = (lat & ~3) + ((lat & 1) << 1) + ((lat & 2) >> 1)
    rows = pl.ds(pl.multiple_of(place * shells, shells), shells)
    cols = slice(chunk * LANES, (chunk + 1) * LANES)
    for parity, value in enumerate((a + b, a - b)):
        high, low = split(value)
        g_ref[parity, 0, rows, cols] = high
        g_ref[parity, 1, rows, cols] = low


def transform(g_ref, t_ref, shells, lats, emit):
    kinds, count, half = t_ref.shape[1:]
    nt = (((1,), (1,)), ((), ()))
    row = lax.broadcasted_iota(jnp.int32, (count, LANES), 0)
    lane = lax.broadcasted_iota(jnp.int32, (count, LANES), 1)
    upper = (row & 7) < 4
    straight = (lane & shells) == 0
    for start, size in ((0, 8), (8, 4)):
        rows = slice(start * shells, (start + size) * shells)
        sums = []
        for parity in range(2):
            table = t_ref[parity].reshape(kinds * count, half)
            high, low = g_ref[parity, 0, rows], g_ref[parity, 1, rows]
            if size == 8:
                main = lax.dot_general(table, high, nt, preferred_element_type=jnp.float32)
                rest = lax.dot_general(
                    table[: 2 * count], low, nt, preferred_element_type=jnp.float32
                )
                sums.append(main[: 2 * count] + main[2 * count :] + rest)
            else:
                both = jnp.concatenate([high, low], axis=0)
                main = lax.dot_general(table, both, nt, preferred_element_type=jnp.float32)
                width = size * shells
                sums.append(
                    main[: 2 * count, :width]
                    + (main[: 2 * count, width:] + main[2 * count :, :width])
                )
        for base in range(0, size, 4):
            cols = slice(base * shells, base * shells + LANES)
            found = []
            for total in sums:
                cosine, sine = total[:count, cols], total[count:, cols]
                found.append(
                    (
                        jnp.where(straight, cosine, pltpu.roll(sine, shells, 1)),
                        jnp.where(straight, pltpu.roll(cosine, LANES - shells, 1), sine),
                    )
                )
            for i in range(2):
                even, odd = found[0][i], found[1][i]
                tiles = (count // 8, 8, LANES)
                emit(
                    (start + base) // 2 + i,
                    jnp.where(upper, even, odd).reshape(tiles),
                    jnp.where(upper, odd, even).reshape(tiles),
                )


def angular_kernel(rho_ref, ang_ref, v_ref, t_ref, a_ref, g_ref):
    lats, shells, lon = v_ref.shape[1:]
    wide = lon // LANES
    scale = shell_rows(shells, lambda r: ang_ref[r] * rho_ref[r])

    def band(lat, _):
        for chunk in range(wide // 2):
            terms = []
            for c in (chunk, chunk + wide // 2):
                cols = slice(c * LANES, (c + 1) * LANES)
                radial, polar, azimuth = (
                    v_ref[k, lat, :, cols].astype(jnp.float32) for k in range(3)
                )
                terms.append(
                    scale
                    * (
                        polar * polar
                        + azimuth * azimuth
                        - 2.0 * radial * radial
                        + polar * azimuth
                    )
                )
            store_folded(g_ref, lat, shells, chunk, *terms)
        return 0

    lax.fori_loop(0, lats, band, 0)

    def emit(pair, left, right):
        a_ref[:, 0, pair] = left
        a_ref[:, 1, pair] = right

    transform(g_ref, t_ref, shells, lats, emit)


def radial_kernel(
    off_ref, rho_ref, w_ref, v_ref, lo_ref, hi_ref, t_ref, a_ref, out_ref, w_rows, c_ref, g_ref, y_ref, out_sem
):
    lats, shells, lon = v_ref.shape[1:]
    wide = lon // LANES
    rho = shell_rows(shells, lambda r: rho_ref[r])
    for tap in range(TAPS):
        for k in range(2):
            w_rows[k, tap] = shell_rows(shells, lambda r: w_ref[k, tap, r])

    def band(lat, _):
        for c in range(wide):
            cols = slice(c * LANES, (c + 1) * LANES)
            radial, polar, azimuth = (
                v_ref[k, lat, :, cols].astype(jnp.float32) for k in range(3)
            )
            flux = rho * radial
            c_ref[0, c, 8 : 8 + shells] = flux * polar
            c_ref[1, c, 8 : 8 + shells] = flux * azimuth
            low, high = lo_ref[lat * wide + c], hi_ref[lat * wide + c]
            c_ref[0, c, 0:8] = low
            c_ref[1, c, 0:8] = pltpu.roll(low, HALO, 0)
            c_ref[0, c, 8 + shells : 16 + shells] = high
            c_ref[1, c, 8 + shells : 16 + shells] = pltpu.roll(high, 8 - HALO, 0)
        for chunk in range(wide // 2):
            terms = []
            for c in (chunk, chunk + wide // 2):
                total = jnp.zeros((shells, LANES), jnp.float32)
                for tap in range(TAPS):
                    at = pl.ds(8 + off_ref[tap], shells)
                    total = (
                        total
                        + w_rows[0, tap] * c_ref[0, c, at, :]
                        + w_rows[1, tap] * c_ref[1, c, at, :]
                    )
                terms.append(total)
            store_folded(g_ref, lat, shells, chunk, *terms)
        return 0

    lax.fori_loop(0, lats, band, 0)

    near = lax.broadcasted_iota(jnp.int32, y_ref.shape[:1] + (8, LANES), 2) < LANES // 2

    def emit(pair, *both):
        for i, mine in enumerate(both):
            other = a_ref[:, i, pair]
            y_ref[:, i, 2 * pair] = jnp.where(near, mine, pltpu.roll(other, LANES // 2, 2))
            y_ref[:, i, 2 * pair + 1] = jnp.where(near, pltpu.roll(mine, LANES // 2, 2), other)
        if pair % 2 == 1:
            out_copy(pair // 2).start()

    def out_copy(i):
        part = pl.ds(4 * i, 4)
        return pltpu.make_async_copy(y_ref.at[:, :, part], out_ref.at[:, :, part], out_sem.at[i])

    transform(g_ref, t_ref, shells, lats, emit)
    for i in range(lats // 4):
        out_copy(i).wait()


def fourier(offsets, density, weights, angular, velocity, below, above, tables):
    _, lats, shells, lon = velocity.shape
    count = tables.shape[2]
    smem = pl.BlockSpec(memory_space=pltpu.SMEM)
    vmem = pl.BlockSpec(memory_space=pltpu.VMEM)
    hbm = pl.BlockSpec(memory_space=pltpu.HBM)
    folded = pltpu.VMEM((2, 2, lats * shells, lon // 2), jnp.bfloat16)
    ready = pl.pallas_call(
        angular_kernel,
        in_specs=[smem, smem, vmem, vmem],
        out_specs=vmem,
        out_shape=jax.ShapeDtypeStruct((count // 8, 2, lats // 2, 8, LANES), jnp.float32),
        scratch_shapes=[folded],
        compiler_params=small(),
        name="angular",
    )(density, angular, velocity, tables)
    return pl.pallas_call(
        radial_kernel,
        in_specs=[smem] * 3 + [vmem] * 5,
        out_specs=hbm,
        out_shape=pltpu.HBM((count // 8, 2, lats, 8, LANES), jnp.float32),
        scratch_shapes=[
            pltpu.VMEM((2, TAPS, shells, LANES), jnp.float32),
            pltpu.VMEM((2, lon // LANES, shells + 16, LANES), jnp.float32),
            folded,
            pltpu.VMEM((count // 8, 2, lats, 8, LANES), jnp.float32),
            pltpu.SemaphoreType.DMA((lats // 4,)),
        ],
        compiler_params=small(),
        name="radial",
    )(
        offsets,
        density,
        weights,
        velocity,
        below,
        above,
        tables,
        ready,
    )


def legendre_kernel(inv_ref, m_ref, start_ref, trig_ref, out_ref, s_ref, p_ref, z_ref, e_ref, x_ref):
    block = x_ref.shape[1] // 8
    pairs = out_ref.shape[1]
    degrees = block * pl.num_programs(0)
    lat_count = trig_ref.shape[1]
    base = pl.program_id(0) * block
    wide = lat_count // LANES
    order = jnp.broadcast_to(m_ref[...], (8, LANES))
    quantum = LEVEL * math.log(2.0)

    def columns(i):
        return slice(i * LANES, (i + 1) * LANES)

    @pl.when(pl.program_id(0) == 0)
    def _():
        start = jnp.broadcast_to(start_ref[...], (8, LANES))
        for i in range(wide):
            log_value = start + order * trig_ref[1:2, columns(i)]
            level = jnp.minimum(jnp.ceil(log_value * (1.0 / quantum)), 0.0)
            z_ref[:, columns(i)] = (
                jnp.exp(log_value - level * quantum) * trig_ref[2:3, columns(i)]
            )
            e_ref[:, columns(i)] = level
        zero = jnp.zeros((8, lat_count), jnp.float32)
        s_ref[...] = zero
        p_ref[...] = zero

    def eight(chunk, _):
        levels, scales, current, older = [], [], [], []
        for i in range(wide):
            s = s_ref[:, columns(i)]
            p = p_ref[:, columns(i)]
            e = e_ref[:, columns(i)]
            grow = (jnp.maximum(jnp.abs(s), jnp.abs(p)) > 1.0) & (e < 0.0)
            shrink = jnp.where(grow, 2.0**-LEVEL, 1.0)
            e = e + jnp.where(grow, 1.0, 0.0)
            e_ref[:, columns(i)] = e
            current.append(s * shrink)
            older.append(p * shrink)
            scales.append(
                jnp.where(
                    e > -0.5,
                    1.0,
                    jnp.where(e > -1.5, 2.0**-LEVEL, jnp.where(e > -2.5, 2.0 ** (-2 * LEVEL), 0.0)),
                )
            )
        first = base + chunk * 8
        before = jnp.maximum(first - 1, 0)
        before_f = before.astype(jnp.float32)
        back = jnp.maximum((before_f * before_f - order * order) * inv_ref[before], 1e-7)
        back = jnp.sqrt(back)
        for step in range(8):
            degree = first + step
            level = degree.astype(jnp.float32)
            ratio = jnp.maximum((level * level - order * order) * inv_ref[degree], 1e-7)
            up = lax.rsqrt(ratio)
            up_back = up * back
            back = ratio * up
            starting = order == level
            for i in range(wide):
                entry = jnp.where(starting, z_ref[:, columns(i)], 0.0) - up_back * older[i]
                value = (up * trig_ref[0:1, columns(i)]) * current[i] + entry
                older[i] = current[i]
                current[i] = value
                x_ref[i, pl.ds(chunk * 8 + step, 8, stride=block), :] = value * scales[i]
        for i in range(wide):
            s_ref[:, columns(i)] = current[i]
            p_ref[:, columns(i)] = older[i]
        return 0

    lax.fori_loop(0, block // 8, eight, 0)

    def keep(o, row):
        rows = pl.ds(pl.multiple_of(row, block), block)
        for i in range(wide):
            high, low = split(x_ref[i, o * block : (o + 1) * block])
            out_ref[0, o % pairs, rows, columns(i)] = high
            out_ref[1, o % pairs, rows, columns(i)] = low

    for o in range(pairs):
        keep(o, base)

    @pl.when(base * 2 >= degrees)
    def _():
        for o in range(pairs, 2 * pairs):
            keep(o, base + degrees // 2)


def in_sent_order(x, dims):
    bits = len(LAT_SPLIT)
    split_bits = x.reshape((2,) * bits + (-1,) + dims)
    order = [LAT_SPLIT.index(name) for name in SENT]
    return split_bits.transpose(order + list(range(bits, split_bits.ndim)))


def legendre_table(orders, lat_count, degrees):
    colatitude = np.pi * (np.arange(lat_count) + 0.5) / lat_count
    colatitude = in_sent_order(colatitude, ()).reshape(-1)
    sine = np.sin(colatitude)
    trig = np.stack(
        [np.cos(colatitude), np.log(sine), math.sqrt(np.pi / lat_count) * sine]
    ).astype(np.float32)
    ladder = np.arange(1, degrees)
    logs = 0.5 * math.log(0.5) + np.concatenate(
        [[0.0], np.cumsum(0.5 * np.log((2.0 * ladder + 1.0) / (2.0 * ladder)))]
    )
    level = np.arange(degrees, dtype=np.float64)
    inverse = (1.0 / np.maximum(4.0 * level * level - 1.0, 1.0)).astype(np.float32)
    start = jnp.take(jnp.asarray(logs, jnp.float32), orders)[:, None]
    block = 64
    shape = (2, 4, degrees * 3 // 2, lat_count)
    vmem = pl.BlockSpec(memory_space=pltpu.VMEM)
    return pl.pallas_call(
        legendre_kernel,
        grid=(degrees // block,),
        in_specs=[pl.BlockSpec(memory_space=pltpu.SMEM), vmem, vmem, vmem],
        out_specs=pl.BlockSpec(shape, lambda i: (0, 0, 0, 0)),
        out_shape=jax.ShapeDtypeStruct(shape, jnp.bfloat16),
        scratch_shapes=[pltpu.VMEM((8, lat_count), jnp.float32)] * 4
        + [pltpu.VMEM((lat_count // LANES, 8 * block, LANES), jnp.float32)],
        compiler_params=small(),
        name="legendre_table",
    )(inverse, orders.astype(jnp.float32)[:, None], start, trig)


DEPTH = 4


def project_kernel(
    m_ref, o_ref, rad_ref, z_ref, t_ref, e_ref, own_ref, far_ref, send_ref, tile_ref, eig_ref, s_ref, q_ref, sem
):
    lat_count = tile_ref.shape[-1]
    block = LANES
    shells, modes, degrees = e_ref.shape
    quarter = modes // 4
    pairs = q_ref.shape[1]
    blocks = degrees // block

    def batch(pair, index, first, to, count):
        return [
            pltpu.make_async_copy(
                t_ref.at[kind, pair, pl.ds(first, count)],
                tile_ref.at[pair, kind, pl.ds(to, count)],
                sem.at[6 * pair + 3 * kind + index],
            )
            for kind in range(2)
        ]

    wide_pair = [m_ref[pair] < block for pair in range(pairs)]
    queue = []
    for pair in range(pairs):
        queue.append(batch(pair, 0, block, block, degrees - block))
        low = pl.multiple_of(jnp.where(wide_pair[pair], 0, degrees), block)
        queue.append(
            batch(pair, 1, low, 0, block)
            + batch(pair, 2, degrees * 3 // 2 - block, degrees, block)
        )
    share = shells // 4
    eigen_copies = [
        pltpu.make_async_copy(
            e_ref.at[pl.ds(i * share, share)],
            eig_ref.at[pl.ds(i * share, share)],
            sem.at[6 * pairs + i],
        )
        for i in range(4)
    ]
    queue.insert(4, eigen_copies)

    def start(i):
        for copy in queue[i] if i < len(queue) else ():
            copy.start()

    def wait(i):
        for copy in queue[i]:
            copy.wait()
        start(i + DEPTH)

    for i in range(DEPTH):
        start(i)
    degree = lax.broadcasted_iota(jnp.int32, (degrees, LANES), 0).astype(jnp.float32)
    factor = degree * (degree + 1.0)

    def sources(pair):
        low, high = (
            jnp.concatenate(split(z_ref[pl.ds(o_ref[i, pair], lat_count, stride=8), :]), axis=1)
            for i in range(2)
        )
        first = jnp.where(wide_pair[pair], factor[:block], factor[degrees // 2 : degrees // 2 + block])
        for part, (data, begin, count, scale) in enumerate(
            (
                (low, block, degrees - block, factor[block:]),
                (jnp.where(wide_pair[pair], low, high), 0, block, first),
                (high, degrees, block, factor[degrees - block :]),
            )
        ):
            number = 2 * pair + min(part, 1)
            if part < 2:
                wait(number if number < 4 else number + 1)
            rows = slice(begin, begin + count)
            main = jnp.dot(tile_ref[pair, 0, rows], data, preferred_element_type=jnp.float32)
            rest = jnp.dot(
                tile_ref[pair, 1, rows], data[:, :LANES], preferred_element_type=jnp.float32
            )
            both = main[:, :LANES] + (main[:, LANES:] + rest)
            source = both - scale * pltpu.roll(both, LANES // 2, 1)
            for i in range(count // block):
                s_ref[pair % 2, begin // block + i] = source[i * block : (i + 1) * block].T

    def modes_of(pair):
        start = pl.multiple_of(jnp.where(wide_pair[pair], 0, degrees // 2), block)
        for place in range(blocks + 1):
            first = start if place == 0 else min(place, blocks - 1) * block
            totals = [jnp.zeros((modes, block), jnp.float32) for _ in range(2)]
            for r in range(shells):
                eigen = eig_ref[r, :, pl.ds(first, block)]
                for part in range(2):
                    row = part * shells + r
                    totals[part] = totals[part] + eigen * s_ref[pair % 2, place, row : row + 1, :]
            for part in range(2):
                for q in range(4):
                    q_ref[q, pair, place, part] = totals[part][q * quarter : (q + 1) * quarter]

    sources(0)
    for pair in range(pairs):
        if pair + 1 < pairs:
            sources(pair + 1)
        if pair == 0:
            wait(4)
        modes_of(pair)
    own_ref[...] = q_ref[rad_ref[0]]
    far_ref[...] = q_ref[rad_ref[0] ^ 2]
    for i in range(2):
        send_ref[i] = q_ref[rad_ref[0] ^ (1 + 2 * i)]


def projected(lower, places, rad, spectrum, table, eigen):
    pairs = lower.shape[0]
    lat_count = table.shape[-1]
    shells, modes, degrees = eigen.shape
    block = LANES
    smem = pl.BlockSpec(memory_space=pltpu.SMEM)
    vmem = pl.BlockSpec(memory_space=pltpu.VMEM)
    hbm = pl.BlockSpec(memory_space=pltpu.HBM)
    shape = (pairs, degrees // block + 1, 2, modes // 4, block)
    return pl.pallas_call(
        project_kernel,
        in_specs=[smem, smem, smem, vmem, hbm, hbm],
        out_specs=[vmem] * 3,
        out_shape=[jax.ShapeDtypeStruct(x, jnp.float32) for x in (shape, shape, (2,) + shape)],
        scratch_shapes=[
            pltpu.VMEM((pairs, 2, degrees + block, lat_count), jnp.bfloat16),
            pltpu.VMEM(eigen.shape, jnp.float32),
            pltpu.VMEM((2, degrees // block + 1, LANES, block), jnp.float32),
            pltpu.VMEM((4,) + shape, jnp.float32),
            pltpu.SemaphoreType.DMA((6 * pairs + 4,)),
        ],
        compiler_params=small(36),
        name="project",
    )(lower, places, rad, spectrum.reshape(lat_count * 8, LANES), table, eigen)


def finish_kernel(m_ref, slot_ref, own_ref, near_ref, far_ref, out_ref):
    pairs, places = own_ref.shape[:2]
    block = own_ref.shape[-1]
    for pair in range(pairs):
        wide_pair = m_ref[pair] < block
        low, high = slot_ref[0, pair], slot_ref[1, pair]

        def total(place):
            return (own_ref[pair, place] + near_ref[0, pair, place]) + far_ref[pair, place]

        first = total(0)
        zero = jnp.zeros_like(first)
        out_ref[low, :, :, 0:block] = jnp.where(wide_pair, first, zero)
        for place in range(1, places - 1):
            out_ref[low, :, :, place * block : (place + 1) * block] = total(place)
        for place in range(places - 3):
            out_ref[high, :, :, place * block : (place + 1) * block] = zero
        out_ref[high, :, :, (places - 3) * block : (places - 2) * block] = jnp.where(
            wide_pair, zero, first
        )
        out_ref[high, :, :, (places - 2) * block :] = total(places - 1)


def finished(lower, slots, own, near, far):
    pairs, places, kinds, modes, block = own.shape
    smem = pl.BlockSpec(memory_space=pltpu.SMEM)
    vmem = pl.BlockSpec(memory_space=pltpu.VMEM)
    return pl.pallas_call(
        finish_kernel,
        in_specs=[smem, smem, vmem, vmem, vmem],
        out_specs=vmem,
        out_shape=jax.ShapeDtypeStruct(
            (2 * pairs, kinds, modes, (places - 1) * block), jnp.float32
        ),
        compiler_params=small(),
        name="finish",
    )(lower, slots, own, near, far)


def body(velocity, density, offsets, radial_weights, angular_scale, order_table, eigenfunctions):
    lats, lon = velocity.shape[2:]
    velocity = jnp.transpose(velocity, (0, 2, 1, 3))
    density, offsets, radial_weights, angular_scale = (
        pltpu.with_memory_space_constraint(x, pltpu.HBM)
        for x in (density, offsets, radial_weights, angular_scale)
    )
    degrees = order_table.shape[0]
    groups = lax.axis_size(SENT)
    size = lax.axis_size("rad")
    lat_count = lats * groups
    where = lax.axis_index(LAT_SPLIT)
    place = lax.axis_index(SENT)

    top, bottom = halo_cross(density, pltpu.with_memory_space_constraint(velocity, pltpu.HBM))
    up = [(i, i + 1) for i in range(size - 1)]
    below = lax.ppermute(top, "rad", up)
    above = lax.ppermute(bottom, "rad", [(j, i) for i, j in up])
    pairs = order_table.reshape(degrees // 2, 2)
    tables = gathered_tables(order_table, master_tables(lon, degrees), lon // 2)
    by_slot = fourier(
        offsets, density, radial_weights, angular_scale, velocity, below, above, tables
    )
    by_slot = by_slot.reshape(groups, lats, 8, LANES)
    gathered = lax.all_to_all(by_slot, SENT, split_axis=0, concat_axis=0, tiled=True)
    gathered = gathered.reshape(lat_count, 8, LANES)

    first = lax.dynamic_slice_in_dim(pairs, where * 4, 4)[:, 0]
    second = degrees - 1 - first
    first_half = (first & 1) == (place & 1)
    eigen = jnp.transpose(eigenfunctions, (2, 1, 0))
    first_low = first < degrees // 2
    lower = jnp.where(first_low, first, second)
    orders = jnp.concatenate([lower, degrees - 1 - lower])
    table = legendre_table(orders, lat_count, degrees)
    number = jnp.arange(4, dtype=jnp.int32)
    slot = 2 * number + jnp.where(first_low, 0, 1)
    slots = jnp.stack([slot, slot ^ 1])
    row = number + jnp.where(first_low == first_half, 0, 4)
    places = jnp.stack([row, row ^ 4])
    rad = lax.axis_index("rad")[None]
    table, eigen = (pltpu.with_memory_space_constraint(x, pltpu.HBM) for x in (table, eigen))
    own, far, send = projected(lower, places, rad, gathered, table, eigen)
    near = lax.ppermute(send, "rad", [(i, i ^ 1) for i in range(size)])
    far = lax.ppermute(far + near[1], "rad", [(i, i ^ 2) for i in range(size)])
    return finished(lower, slots, own, near, far)


def solution(mesh):
    bits = len(LAT_SPLIT)
    mesh = jax.sharding.Mesh(
        mesh.devices.reshape((-1,) + (2,) * bits), ("rad",) + LAT_SPLIT
    )
    placed = (
        P(None, "rad", LAT_SPLIT, None),
        P("rad"),
        P(),
        P(None, None, "rad"),
        P("rad"),
        P(),
        P(None, None, "rad"),
    )
    return jax.shard_map(
        body, mesh=mesh, in_specs=placed, out_specs=P(LAT_SPLIT, None, "rad", None), check_vma=False
    )
```

```python
import math

import jax
import jax.numpy as jnp
import numpy as np
from jax import lax
from jax.experimental import pallas as pl
from jax.experimental.pallas import tpu as pltpu
from jax.sharding import PartitionSpec as P


TAPS = 4
HALO = 3
LANES = 128
LAT_SPLIT = ("x", "z2", "z1", "z0", "y1", "y0")
SENT = LAT_SPLIT
LEVEL = 60.0


def master_tables(lon, degrees):
    orders = np.arange(degrees).reshape(degrees // 2, 2).T[:, :, None]
    fine = (2.0 * np.pi / lon) * ((orders * np.arange(LANES)) % lon)
    coarse = (2.0 * np.pi / lon) * ((orders * LANES * np.arange(lon // 2 // LANES)) % lon)
    turns = np.concatenate([np.cos(coarse), np.sin(coarse)], axis=2)
    turns = np.pad(turns, ((0, 0), (0, 0), (0, LANES - turns.shape[2])))
    rest = np.concatenate(
        [np.cos(fine) / math.sqrt(lon), np.sin(fine) / math.sqrt(lon), turns], axis=2
    )
    terms = []
    for _ in range(3):
        terms.append(rest.astype(np.float32).astype(jnp.bfloat16))
        rest = rest - terms[-1].astype(np.float64)
    return np.concatenate(terms, axis=2)


def small(mebibytes=24):
    return pltpu.CompilerParams(vmem_limit_bytes=mebibytes * 2**20)


def split(x):
    high = x.astype(jnp.bfloat16)
    return high, (x - high.astype(jnp.float32)).astype(jnp.bfloat16)


def gather_kernel(first_ref, table_ref, out_ref):
    count = table_ref.shape[1]
    spot = lax.broadcasted_iota(jnp.int32, (1, LANES), 1)
    halves = []
    for base in range(0, count, LANES):
        half = jnp.zeros((1, LANES), jnp.int32)
        for i in range(LANES):
            half = jnp.where(spot == i, first_ref[2 * (base + i)], half)
        halves.append(half)
    first = jnp.concatenate(halves, axis=1)
    even = jnp.where((first & 1) == 0, first, 2 * count - 1 - first)
    odd = 2 * count - 1 - even
    lane = lax.broadcasted_iota(jnp.int32, (1, count), 1)
    swapped = jnp.where((lane & 4) == 0, pltpu.roll(odd, count - 4, 1), pltpu.roll(odd, 4, 1))
    wide = table_ref.shape[2] // 3
    steps = out_ref.shape[-1] // LANES
    for parity, orders in enumerate((even, swapped)):
        row = orders >> 1
        hot = (lax.broadcasted_iota(jnp.int32, (count, count), 0) == row).astype(jnp.float32)
        hot = hot.T.astype(jnp.bfloat16)
        terms = jnp.dot(hot, table_ref[parity], preferred_element_type=jnp.float32)
        found = terms[:, :wide] + (terms[:, wide : 2 * wide] + terms[:, 2 * wide :])
        cosine, sine, turns = (found[:, i * LANES : (i + 1) * LANES] for i in range(3))
        for a in range(steps):
            c, s = (
                jnp.broadcast_to(turns[:, i : i + 1], (count, LANES)) for i in (a, steps + a)
            )
            cols = slice(a * LANES, (a + 1) * LANES)
            for part, value in enumerate((c * cosine - s * sine, -(s * cosine + c * sine))):
                high, low = split(value)
                out_ref[parity, part, :, cols] = high
                out_ref[parity, 2 + part, :, cols] = low


def gathered_tables(first, tables, half):
    vmem = pl.BlockSpec(memory_space=pltpu.VMEM)
    return pl.pallas_call(
        gather_kernel,
        in_specs=[pl.BlockSpec(memory_space=pltpu.SMEM), vmem],
        out_specs=vmem,
        out_shape=jax.ShapeDtypeStruct((2, 4, tables.shape[1], half), jnp.bfloat16),
        compiler_params=small(),
        name="gather_rows",
    )(first, tables)


def halo_kernel(rho_ref, v_ref, top_ref, bottom_ref, flow_ref, sem):
    lats, shells, lon = v_ref.shape[1:]
    starts = (shells - 8, 0)
    copies = [
        [
            pltpu.make_async_copy(
                v_ref.at[k, :, pl.ds(start, 8)], flow_ref.at[i, k], sem.at[3 * i + k]
            )
            for k in range(3)
        ]
        for i, start in enumerate(starts)
    ]
    for side in copies:
        for copy in side:
            copy.start()
    wide = lon // LANES
    row = lax.broadcasted_iota(jnp.int32, (8, LANES), 0)
    for i, (start, out_ref) in enumerate(zip(starts, (top_ref, bottom_ref))):
        mine = row >= 8 - HALO if i == 0 else row < HALO
        away = 8 - HALO if i == 0 else HALO
        rho = jnp.zeros((8, LANES), jnp.float32)
        for h in range(8):
            rho = jnp.where(row == h, rho_ref[start + h], rho)
        for copy in copies[i]:
            copy.wait()

        def band(lat, _, i=i, rho=rho, out_ref=out_ref, mine=mine, away=away):
            for c in range(wide):
                cols = slice(c * LANES, (c + 1) * LANES)
                radial, polar, azimuth = (
                    flow_ref[i, k, lat, :, cols].astype(jnp.float32) for k in range(3)
                )
                flux = rho * radial
                other = pltpu.roll(flux * azimuth, away, 0)
                out_ref[lat * wide + c] = jnp.where(mine, flux * polar, other)
            return 0

        lax.fori_loop(0, lats, band, 0)


def halo_cross(density, velocity):
    _, lats, shells, lon = velocity.shape
    vmem = pl.BlockSpec(memory_space=pltpu.VMEM)
    shape = jax.ShapeDtypeStruct((lats * lon // LANES, 8, LANES), jnp.float32)
    return pl.pallas_call(
        halo_kernel,
        in_specs=[pl.BlockSpec(memory_space=pltpu.SMEM), pl.BlockSpec(memory_space=pltpu.HBM)],
        out_specs=[vmem, vmem],
        out_shape=[shape, shape],
        scratch_shapes=[
            pltpu.VMEM((2, 3, lats, 8, lon), jnp.bfloat16),
            pltpu.SemaphoreType.DMA((6,)),
        ],
        compiler_params=small(),
        name="halo_cross",
    )(density, velocity)


def shell_rows(count, value):
    row = lax.broadcasted_iota(jnp.int32, (8, LANES), 0)
    tiles = []
    for base in range(0, count, 8):
        tile = jnp.zeros((8, LANES), jnp.float32)
        for h in range(8):
            tile = jnp.where(row == h, value(base + h), tile)
        tiles.append(tile)
    return jnp.concatenate(tiles, axis=0)


def store_folded(g_ref, lat, shells, chunk, a, b):
    place = (lat & ~3) + ((lat & 1) << 1) + ((lat & 2) >> 1)
    rows = pl.ds(pl.multiple_of(place * shells, shells), shells)
    cols = slice(chunk * LANES, (chunk + 1) * LANES)
    for parity, value in enumerate((a + b, a - b)):
        high, low = split(value)
        g_ref[parity, 0, rows, cols] = high
        g_ref[parity, 1, rows, cols] = low


def transform(g_ref, t_ref, shells, lats, emit):
    kinds, count, half = t_ref.shape[1:]
    nt = (((1,), (1,)), ((), ()))
    row = lax.broadcasted_iota(jnp.int32, (count, LANES), 0)
    lane = lax.broadcasted_iota(jnp.int32, (count, LANES), 1)
    upper = (row & 7) < 4
    straight = (lane & shells) == 0
    for start, size in ((0, 8), (8, 4)):
        rows = slice(start * shells, (start + size) * shells)
        sums = []
        for parity in range(2):
            table = t_ref[parity].reshape(kinds * count, half)
            high, low = g_ref[parity, 0, rows], g_ref[parity, 1, rows]
            if size == 8:
                main = lax.dot_general(table, high, nt, preferred_element_type=jnp.float32)
                rest = lax.dot_general(
                    table[: 2 * count], low, nt, preferred_element_type=jnp.float32
                )
                sums.append(main[: 2 * count] + main[2 * count :] + rest)
            else:
                both = jnp.concatenate([high, low], axis=0)
                main = lax.dot_general(table, both, nt, preferred_element_type=jnp.float32)
                width = size * shells
                sums.append(
                    main[: 2 * count, :width]
                    + (main[: 2 * count, width:] + main[2 * count :, :width])
                )
        for base in range(0, size, 4):
            cols = slice(base * shells, base * shells + LANES)
            found = []
            for total in sums:
                cosine, sine = total[:count, cols], total[count:, cols]
                found.append(
                    (
                        jnp.where(straight, cosine, pltpu.roll(sine, shells, 1)),
                        jnp.where(straight, pltpu.roll(cosine, LANES - shells, 1), sine),
                    )
                )
            for i in range(2):
                even, odd = found[0][i], found[1][i]
                tiles = (count // 8, 8, LANES)
                emit(
                    (start + base) // 2 + i,
                    jnp.where(upper, even, odd).reshape(tiles),
                    jnp.where(upper, odd, even).reshape(tiles),
                )


def angular_kernel(rho_ref, ang_ref, v_ref, t_ref, a_ref, g_ref):
    lats, shells, lon = v_ref.shape[1:]
    wide = lon // LANES
    scale = shell_rows(shells, lambda r: ang_ref[r] * rho_ref[r])

    def band(lat, _):
        for chunk in range(wide // 2):
            terms = []
            for c in (chunk, chunk + wide // 2):
                cols = slice(c * LANES, (c + 1) * LANES)
                radial, polar, azimuth = (
                    v_ref[k, lat, :, cols].astype(jnp.float32) for k in range(3)
                )
                terms.append(
                    scale
                    * (
                        polar * polar
                        + azimuth * azimuth
                        - 2.0 * radial * radial
                        + polar * azimuth
                    )
                )
            store_folded(g_ref, lat, shells, chunk, *terms)
        return 0

    lax.fori_loop(0, lats, band, 0)

    def emit(pair, left, right):
        a_ref[:, 0, pair] = left
        a_ref[:, 1, pair] = right

    transform(g_ref, t_ref, shells, lats, emit)


def radial_kernel(
    off_ref, rho_ref, w_ref, v_ref, lo_ref, hi_ref, t_ref, a_ref, out_ref, w_rows, c_ref, g_ref, y_ref, out_sem
):
    lats, shells, lon = v_ref.shape[1:]
    wide = lon // LANES
    rho = shell_rows(shells, lambda r: rho_ref[r])
    for tap in range(TAPS):
        for k in range(2):
            w_rows[k, tap] = shell_rows(shells, lambda r: w_ref[k, tap, r])

    def band(lat, _):
        for c in range(wide):
            cols = slice(c * LANES, (c + 1) * LANES)
            radial, polar, azimuth = (
                v_ref[k, lat, :, cols].astype(jnp.float32) for k in range(3)
            )
            flux = rho * radial
            c_ref[0, c, 8 : 8 + shells] = flux * polar
            c_ref[1, c, 8 : 8 + shells] = flux * azimuth
            low, high = lo_ref[lat * wide + c], hi_ref[lat * wide + c]
            c_ref[0, c, 0:8] = low
            c_ref[1, c, 0:8] = pltpu.roll(low, HALO, 0)
            c_ref[0, c, 8 + shells : 16 + shells] = high
            c_ref[1, c, 8 + shells : 16 + shells] = pltpu.roll(high, 8 - HALO, 0)
        for chunk in range(wide // 2):
            terms = []
            for c in (chunk, chunk + wide // 2):
                total = jnp.zeros((shells, LANES), jnp.float32)
                for tap in range(TAPS):
                    at = pl.ds(8 + off_ref[tap], shells)
                    total = (
                        total
                        + w_rows[0, tap] * c_ref[0, c, at, :]
                        + w_rows[1, tap] * c_ref[1, c, at, :]
                    )
                terms.append(total)
            store_folded(g_ref, lat, shells, chunk, *terms)
        return 0

    lax.fori_loop(0, lats, band, 0)

    near = lax.broadcasted_iota(jnp.int32, y_ref.shape[:1] + (8, LANES), 2) < LANES // 2

    def emit(pair, *both):
        for i, mine in enumerate(both):
            other = a_ref[:, i, pair]
            y_ref[:, i, 2 * pair] = jnp.where(near, mine, pltpu.roll(other, LANES // 2, 2))
            y_ref[:, i, 2 * pair + 1] = jnp.where(near, pltpu.roll(mine, LANES // 2, 2), other)
        if pair % 2 == 1:
            out_copy(pair // 2).start()

    def out_copy(i):
        part = pl.ds(4 * i, 4)
        return pltpu.make_async_copy(y_ref.at[:, :, part], out_ref.at[:, :, part], out_sem.at[i])

    transform(g_ref, t_ref, shells, lats, emit)
    for i in range(lats // 4):
        out_copy(i).wait()


def fourier(offsets, density, weights, angular, velocity, below, above, tables):
    _, lats, shells, lon = velocity.shape
    count = tables.shape[2]
    smem = pl.BlockSpec(memory_space=pltpu.SMEM)
    vmem = pl.BlockSpec(memory_space=pltpu.VMEM)
    hbm = pl.BlockSpec(memory_space=pltpu.HBM)
    folded = pltpu.VMEM((2, 2, lats * shells, lon // 2), jnp.bfloat16)
    ready = pl.pallas_call(
        angular_kernel,
        in_specs=[smem, smem, vmem, vmem],
        out_specs=vmem,
        out_shape=jax.ShapeDtypeStruct((count // 8, 2, lats // 2, 8, LANES), jnp.float32),
        scratch_shapes=[folded],
        compiler_params=small(),
        name="angular",
    )(density, angular, velocity, tables)
    return pl.pallas_call(
        radial_kernel,
        in_specs=[smem] * 3 + [vmem] * 5,
        out_specs=hbm,
        out_shape=pltpu.HBM((count // 8, 2, lats, 8, LANES), jnp.float32),
        scratch_shapes=[
            pltpu.VMEM((2, TAPS, shells, LANES), jnp.float32),
            pltpu.VMEM((2, lon // LANES, shells + 16, LANES), jnp.float32),
            folded,
            pltpu.VMEM((count // 8, 2, lats, 8, LANES), jnp.float32),
            pltpu.SemaphoreType.DMA((lats // 4,)),
        ],
        compiler_params=small(),
        name="radial",
    )(
        offsets,
        density,
        weights,
        velocity,
        below,
        above,
        tables,
        ready,
    )


def legendre_kernel(inv_ref, m_ref, start_ref, trig_ref, out_ref, s_ref, p_ref, z_ref, e_ref, x_ref):
    block = x_ref.shape[1] // 8
    pairs = out_ref.shape[1]
    degrees = block * pl.num_programs(0)
    lat_count = trig_ref.shape[1]
    base = pl.program_id(0) * block
    wide = lat_count // LANES
    order = jnp.broadcast_to(m_ref[...], (8, LANES))
    quantum = LEVEL * math.log(2.0)

    def columns(i):
        return slice(i * LANES, (i + 1) * LANES)

    @pl.when(pl.program_id(0) == 0)
    def _():
        start = jnp.broadcast_to(start_ref[...], (8, LANES))
        for i in range(wide):
            log_value = start + order * trig_ref[1:2, columns(i)]
            level = jnp.minimum(jnp.ceil(log_value * (1.0 / quantum)), 0.0)
            z_ref[:, columns(i)] = (
                jnp.exp(log_value - level * quantum) * trig_ref[2:3, columns(i)]
            )
            e_ref[:, columns(i)] = level
        zero = jnp.zeros((8, lat_count), jnp.float32)
        s_ref[...] = zero
        p_ref[...] = zero

    def eight(chunk, _):
        levels, scales, current, older = [], [], [], []
        for i in range(wide):
            s = s_ref[:, columns(i)]
            p = p_ref[:, columns(i)]
            e = e_ref[:, columns(i)]
            grow = (jnp.maximum(jnp.abs(s), jnp.abs(p)) > 1.0) & (e < 0.0)
            shrink = jnp.where(grow, 2.0**-LEVEL, 1.0)
            e = e + jnp.where(grow, 1.0, 0.0)
            e_ref[:, columns(i)] = e
            current.append(s * shrink)
            older.append(p * shrink)
            scales.append(
                jnp.where(
                    e > -0.5,
                    1.0,
                    jnp.where(e > -1.5, 2.0**-LEVEL, jnp.where(e > -2.5, 2.0 ** (-2 * LEVEL), 0.0)),
                )
            )
        first = base + chunk * 8
        before = jnp.maximum(first - 1, 0)
        before_f = before.astype(jnp.float32)
        back = jnp.maximum((before_f * before_f - order * order) * inv_ref[before], 1e-7)
        back = jnp.sqrt(back)
        for step in range(8):
            degree = first + step
            level = degree.astype(jnp.float32)
            ratio = jnp.maximum((level * level - order * order) * inv_ref[degree], 1e-7)
            up = lax.rsqrt(ratio)
            up_back = up * back
            back = ratio * up
            starting = order == level
            for i in range(wide):
                entry = jnp.where(starting, z_ref[:, columns(i)], 0.0) - up_back * older[i]
                value = (up * trig_ref[0:1, columns(i)]) * current[i] + entry
                older[i] = current[i]
                current[i] = value
                x_ref[i, pl.ds(chunk * 8 + step, 8, stride=block), :] = value * scales[i]
        for i in range(wide):
            s_ref[:, columns(i)] = current[i]
            p_ref[:, columns(i)] = older[i]
        return 0

    lax.fori_loop(0, block // 8, eight, 0)

    def keep(o, row):
        rows = pl.ds(pl.multiple_of(row, block), block)
        for i in range(wide):
            high, low = split(x_ref[i, o * block : (o + 1) * block])
            out_ref[0, o % pairs, rows, columns(i)] = high
            out_ref[1, o % pairs, rows, columns(i)] = low

    for o in range(pairs):
        keep(o, base)

    @pl.when(base * 2 >= degrees)
    def _():
        for o in range(pairs, 2 * pairs):
            keep(o, base + degrees // 2)


def in_sent_order(x, dims):
    bits = len(LAT_SPLIT)
    split_bits = x.reshape((2,) * bits + (-1,) + dims)
    order = [LAT_SPLIT.index(name) for name in SENT]
    return split_bits.transpose(order + list(range(bits, split_bits.ndim)))


def legendre_table(orders, lat_count, degrees):
    colatitude = np.pi * (np.arange(lat_count) + 0.5) / lat_count
    colatitude = in_sent_order(colatitude, ()).reshape(-1)
    sine = np.sin(colatitude)
    trig = np.stack(
        [np.cos(colatitude), np.log(sine), math.sqrt(np.pi / lat_count) * sine]
    ).astype(np.float32)
    ladder = np.arange(1, degrees)
    logs = 0.5 * math.log(0.5) + np.concatenate(
        [[0.0], np.cumsum(0.5 * np.log((2.0 * ladder + 1.0) / (2.0 * ladder)))]
    )
    level = np.arange(degrees, dtype=np.float64)
    inverse = (1.0 / np.maximum(4.0 * level * level - 1.0, 1.0)).astype(np.float32)
    start = jnp.take(jnp.asarray(logs, jnp.float32), orders)[:, None]
    block = 64
    shape = (2, 4, degrees * 3 // 2, lat_count)
    vmem = pl.BlockSpec(memory_space=pltpu.VMEM)
    return pl.pallas_call(
        legendre_kernel,
        grid=(degrees // block,),
        in_specs=[pl.BlockSpec(memory_space=pltpu.SMEM), vmem, vmem, vmem],
        out_specs=pl.BlockSpec(shape, lambda i: (0, 0, 0, 0)),
        out_shape=jax.ShapeDtypeStruct(shape, jnp.bfloat16),
        scratch_shapes=[pltpu.VMEM((8, lat_count), jnp.float32)] * 4
        + [pltpu.VMEM((lat_count // LANES, 8 * block, LANES), jnp.float32)],
        compiler_params=small(),
        name="legendre_table",
    )(inverse, orders.astype(jnp.float32)[:, None], start, trig)


DEPTH = 9


def project_kernel(
    m_ref, o_ref, rad_ref, z_ref, t_ref, e_ref, own_ref, far_ref, send_ref, tile_ref, eig_ref, s_ref, q_ref, sem
):
    lat_count = tile_ref.shape[-1]
    block = LANES
    shells, modes, degrees = e_ref.shape
    quarter = modes // 4
    pairs = q_ref.shape[1]
    blocks = degrees // block

    def batch(pair, index, first, to, count):
        return [
            pltpu.make_async_copy(
                t_ref.at[kind, pair, pl.ds(first, count)],
                tile_ref.at[pair, kind, pl.ds(to, count)],
                sem.at[6 * pair + 3 * kind + index],
            )
            for kind in range(2)
        ]

    wide_pair = [m_ref[pair] < block for pair in range(pairs)]
    queue = []
    for pair in range(pairs):
        queue.append(batch(pair, 0, block, block, degrees - block))
        low = pl.multiple_of(jnp.where(wide_pair[pair], 0, degrees), block)
        queue.append(
            batch(pair, 1, low, 0, block)
            + batch(pair, 2, degrees * 3 // 2 - block, degrees, block)
        )
    share = shells // 4
    eigen_copies = [
        pltpu.make_async_copy(
            e_ref.at[pl.ds(i * share, share)],
            eig_ref.at[pl.ds(i * share, share)],
            sem.at[6 * pairs + i],
        )
        for i in range(4)
    ]
    queue.insert(4, eigen_copies)

    def start(i):
        for copy in queue[i] if i < len(queue) else ():
            copy.start()

    def wait(i):
        for copy in queue[i]:
            copy.wait()
        start(i + DEPTH)

    for i in range(DEPTH):
        start(i)
    degree = lax.broadcasted_iota(jnp.int32, (degrees, LANES), 0).astype(jnp.float32)
    factor = degree * (degree + 1.0)

    def sources(pair):
        low, high = (
            jnp.concatenate(split(z_ref[pl.ds(o_ref[i, pair], lat_count, stride=8), :]), axis=1)
            for i in range(2)
        )
        first = jnp.where(wide_pair[pair], factor[:block], factor[degrees // 2 : degrees // 2 + block])
        for part, (data, begin, count, scale) in enumerate(
            (
                (low, block, degrees - block, factor[block:]),
                (jnp.where(wide_pair[pair], low, high), 0, block, first),
                (high, degrees, block, factor[degrees - block :]),
            )
        ):
            number = 2 * pair + min(part, 1)
            if part < 2:
                wait(number if number < 4 else number + 1)
            rows = slice(begin, begin + count)
            main = jnp.dot(tile_ref[pair, 0, rows], data, preferred_element_type=jnp.float32)
            rest = jnp.dot(
                tile_ref[pair, 1, rows], data[:, :LANES], preferred_element_type=jnp.float32
            )
            both = main[:, :LANES] + (main[:, LANES:] + rest)
            source = both - scale * pltpu.roll(both, LANES // 2, 1)
            for i in range(count // block):
                s_ref[pair % 2, begin // block + i] = source[i * block : (i + 1) * block].T

    def modes_of(pair):
        start = pl.multiple_of(jnp.where(wide_pair[pair], 0, degrees // 2), block)
        for place in range(blocks + 1):
            first = start if place == 0 else min(place, blocks - 1) * block
            totals = [jnp.zeros((modes, block), jnp.float32) for _ in range(2)]
            for r in range(shells):
                eigen = eig_ref[r, :, pl.ds(first, block)]
                for part in range(2):
                    row = part * shells + r
                    totals[part] = totals[part] + eigen * s_ref[pair % 2, place, row : row + 1, :]
            for part in range(2):
                for q in range(4):
                    q_ref[q, pair, place, part] = totals[part][q * quarter : (q + 1) * quarter]

    sources(0)
    for pair in range(pairs):
        if pair + 1 < pairs:
            sources(pair + 1)
        if pair == 0:
            wait(4)
        modes_of(pair)
    own_ref[...] = q_ref[rad_ref[0]]
    far_ref[...] = q_ref[rad_ref[0] ^ 2]
    for i in range(2):
        send_ref[i] = q_ref[rad_ref[0] ^ (1 + 2 * i)]


def projected(lower, places, rad, spectrum, table, eigen):
    pairs = lower.shape[0]
    lat_count = table.shape[-1]
    shells, modes, degrees = eigen.shape
    block = LANES
    smem = pl.BlockSpec(memory_space=pltpu.SMEM)
    vmem = pl.BlockSpec(memory_space=pltpu.VMEM)
    hbm = pl.BlockSpec(memory_space=pltpu.HBM)
    shape = (pairs, degrees // block + 1, 2, modes // 4, block)
    return pl.pallas_call(
        project_kernel,
        in_specs=[smem, smem, smem, vmem, hbm, hbm],
        out_specs=[vmem] * 3,
        out_shape=[jax.ShapeDtypeStruct(x, jnp.float32) for x in (shape, shape, (2,) + shape)],
        scratch_shapes=[
            pltpu.VMEM((pairs, 2, degrees + block, lat_count), jnp.bfloat16),
            pltpu.VMEM(eigen.shape, jnp.float32),
            pltpu.VMEM((2, degrees // block + 1, LANES, block), jnp.float32),
            pltpu.VMEM((4,) + shape, jnp.float32),
            pltpu.SemaphoreType.DMA((6 * pairs + 4,)),
        ],
        compiler_params=small(36),
        name="project",
    )(lower, places, rad, spectrum.reshape(lat_count * 8, LANES), table, eigen)


def finish_kernel(m_ref, slot_ref, own_ref, near_ref, far_ref, out_ref):
    pairs, places = own_ref.shape[:2]
    block = own_ref.shape[-1]
    for pair in range(pairs):
        wide_pair = m_ref[pair] < block
        low, high = slot_ref[0, pair], slot_ref[1, pair]

        def total(place):
            return (own_ref[pair, place] + near_ref[0, pair, place]) + far_ref[pair, place]

        first = total(0)
        zero = jnp.zeros_like(first)
        out_ref[low, :, :, 0:block] = jnp.where(wide_pair, first, zero)
        for place in range(1, places - 1):
            out_ref[low, :, :, place * block : (place + 1) * block] = total(place)
        for place in range(places - 3):
            out_ref[high, :, :, place * block : (place + 1) * block] = zero
        out_ref[high, :, :, (places - 3) * block : (places - 2) * block] = jnp.where(
            wide_pair, zero, first
        )
        out_ref[high, :, :, (places - 2) * block :] = total(places - 1)


def finished(lower, slots, own, near, far):
    pairs, places, kinds, modes, block = own.shape
    smem = pl.BlockSpec(memory_space=pltpu.SMEM)
    vmem = pl.BlockSpec(memory_space=pltpu.VMEM)
    return pl.pallas_call(
        finish_kernel,
        in_specs=[smem, smem, vmem, vmem, vmem],
        out_specs=vmem,
        out_shape=jax.ShapeDtypeStruct(
            (2 * pairs, kinds, modes, (places - 1) * block), jnp.float32
        ),
        compiler_params=small(),
        name="finish",
    )(lower, slots, own, near, far)


def body(velocity, density, offsets, radial_weights, angular_scale, order_table, eigenfunctions):
    lats, lon = velocity.shape[2:]
    velocity = jnp.transpose(velocity, (0, 2, 1, 3))
    density, offsets, radial_weights, angular_scale = (
        pltpu.with_memory_space_constraint(x, pltpu.HBM)
        for x in (density, offsets, radial_weights, angular_scale)
    )
    degrees = order_table.shape[0]
    groups = lax.axis_size(SENT)
    size = lax.axis_size("rad")
    lat_count = lats * groups
    where = lax.axis_index(LAT_SPLIT)
    place = lax.axis_index(SENT)

    top, bottom = halo_cross(density, pltpu.with_memory_space_constraint(velocity, pltpu.HBM))
    up = [(i, i + 1) for i in range(size - 1)]
    below = lax.ppermute(top, "rad", up)
    above = lax.ppermute(bottom, "rad", [(j, i) for i, j in up])
    pairs = order_table.reshape(degrees // 2, 2)
    tables = gathered_tables(order_table, master_tables(lon, degrees), lon // 2)
    by_slot = fourier(
        offsets, density, radial_weights, angular_scale, velocity, below, above, tables
    )
    by_slot = by_slot.reshape(groups, lats, 8, LANES)
    gathered = lax.all_to_all(by_slot, SENT, split_axis=0, concat_axis=0, tiled=True)
    gathered = gathered.reshape(lat_count, 8, LANES)

    first = lax.dynamic_slice_in_dim(pairs, where * 4, 4)[:, 0]
    second = degrees - 1 - first
    first_half = (first & 1) == (place & 1)
    eigen = jnp.transpose(eigenfunctions, (2, 1, 0))
    first_low = first < degrees // 2
    lower = jnp.where(first_low, first, second)
    orders = jnp.concatenate([lower, degrees - 1 - lower])
    table = legendre_table(orders, lat_count, degrees)
    number = jnp.arange(4, dtype=jnp.int32)
    slot = 2 * number + jnp.where(first_low, 0, 1)
    slots = jnp.stack([slot, slot ^ 1])
    row = number + jnp.where(first_low == first_half, 0, 4)
    places = jnp.stack([row, row ^ 4])
    rad = lax.axis_index("rad")[None]
    table, eigen = (pltpu.with_memory_space_constraint(x, pltpu.HBM) for x in (table, eigen))
    own, far, send = projected(lower, places, rad, gathered, table, eigen)
    near = lax.ppermute(send, "rad", [(i, i ^ 1) for i in range(size)])
    far = lax.ppermute(far + near[1], "rad", [(i, i ^ 2) for i in range(size)])
    return finished(lower, slots, own, near, far)


def solution(mesh):
    bits = len(LAT_SPLIT)
    mesh = jax.sharding.Mesh(
        mesh.devices.reshape((-1,) + (2,) * bits), ("rad",) + LAT_SPLIT
    )
    placed = (
        P(None, "rad", LAT_SPLIT, None),
        P("rad"),
        P(),
        P(None, None, "rad"),
        P("rad"),
        P(),
        P(None, None, "rad"),
    )
    return jax.shard_map(
        body, mesh=mesh, in_specs=placed, out_specs=P(LAT_SPLIT, None, "rad", None), check_vma=False
    )
```
